256 devices in a mesh: line: 4 (over x), cross: 64 (over y, z, core).
Axes of the slice: x: 4, y: 4, z: 8, core: 2. Of those that a mesh axis runs over, the one named last changes fastest.
Arguments:
- velocity: float32 [3, 512, 512, 256], P(None, 'line', 'cross'), may hold values from -6 to 6
Outputs:
- advection: float32 [3, 512, 512, 256], P(None, 'line', 'cross')
- x_derivative: float32 [3, 512, 512, 256], P(None, 'line', 'cross')
The draws below stay inside these ranges and needn't reach their ends.
All inputs are finite; a program needn't handle non-finite values.
Results may differ from the reference program's by a relative error of at most 0.0001.
Values sent between devices are 32-bit elements; how exact they have to be, the bound alone decides.
No kernel may reach another device: no remote copies, remote signals or barrier semaphores. Data moves between devices by JAX's collectives and lax.ppermute only.
A program may use at most 128 MiB of HBM per device.

```python
import math
import jax
import jax.numpy as jnp

NX = 512
NZ = 256
NY = 512


def shard_levels(own_key, shape, shards, low, top_value):
    def one(position, blocks):
        heights = jax.random.uniform(jax.random.fold_in(jax.random.fold_in(own_key, 6), position), (blocks,), jnp.float32, low / len(shards), top_value / len(shards))
        return jnp.repeat(jnp.exp(heights), shape[position] // blocks).reshape((-1,) + (1,) * (len(shape) - position - 1))

    loudness = one(*shards[0])
    for cut in shards[1:]:
        loudness = loudness * one(*cut)
    return loudness


def noise(own_key, shape, deviation, bound, split=(), held_as=jnp.bfloat16):
    values = deviation * jax.random.normal(own_key, shape, jnp.float32)
    if split:
        values = values * shard_levels(own_key, shape, split, -0.22, 0.18)
    return jnp.clip(values, -bound, bound).astype(held_as)


def setup_inputs(seed: int = 0) -> dict:
    seeds = jax.random.split(jax.random.key(seed), 2)
    velocity = noise(seeds[0], (3, NX, NY, NZ), 1.0, 6.0, ((1, 4), (2, 64)), jnp.float32)
    return {"velocity": velocity}


ALPHA = 1.0 / 3.0
COEF_A = 14.0 / 9.0
COEF_B = 1.0 / 9.0


def explicit_sixth(field, axis):
    total = 45.0 * (jnp.roll(field, -1, axis) - jnp.roll(field, 1, axis))
    total = total - 9.0 * (jnp.roll(field, -2, axis) - jnp.roll(field, 2, axis))
    total = total + (jnp.roll(field, -3, axis) - jnp.roll(field, 3, axis))
    return total / 60.0


def compact_x(field):
    waves = 2.0 * math.pi * jnp.arange(NX // 2 + 1).astype(jnp.float32) / NX
    factor = (COEF_A * jnp.sin(waves) + 0.5 * COEF_B * jnp.sin(2.0 * waves)) / (1.0 + 2.0 * ALPHA * jnp.cos(waves))
    spectrum = jnp.fft.rfft(field, axis=0)
    result = jnp.fft.irfft(spectrum * (1j * factor)[:, None, None], n=NX, axis=0)
    return result.astype(field.dtype)


def reference(velocity):
    speed_u, speed_v, speed_w = velocity[0], velocity[1], velocity[2]
    advected = []
    derived = []
    for comp in range(3):
        field = velocity[comp]
        along_x = compact_x(field)
        along_y = explicit_sixth(field, 1)
        along_z = explicit_sixth(field, 2)
        advected.append(-(speed_u * along_x + speed_v * along_y + speed_w * along_z))
        derived.append(along_x)
    return jnp.stack(advected), jnp.stack(derived)
```

```python
import functools

import jax
import jax.numpy as jnp
import numpy as np
from jax import lax
from jax.experimental import pallas as pl
from jax.experimental.pallas import tpu as pltpu
from jax.sharding import PartitionSpec as P

ALPHA = 1.0 / 3.0
ROOT = (-1.0 + np.sqrt(1.0 - 4.0 * ALPHA * ALPHA)) / (2.0 * ALPHA)
KAPPA = -ALPHA / ROOT
NEAR = float(7.0 / 9.0 / KAPPA)
FAR = float(1.0 / 36.0 / KAPPA)
R = float(ROOT)
GAIN = float(1.0 / (1.0 - ROOT * ROOT))
TAPS = {1: 45.0, 2: -9.0, 3: 1.0, -1: -45.0, -2: 9.0, -3: -1.0}
CHUNKS = 1
XB = 32


def z_matrix(n):
    m = np.zeros((n, n), np.float32)
    for k, t in TAPS.items():
        for z in range(n):
            m[(z + k) % n, z] += t
    return m


def y_matrix(tile, xb):
    m = np.zeros((tile, tile), np.float32)
    for k, t in TAPS.items():
        for y in range(tile):
            if 0 <= y + k < tile:
                m[y, y + k] += t
    return np.kron(np.eye(xb, dtype=np.float32), m)


def halo_matrix(tile, xb):
    m = np.zeros((xb, tile, 2, 3, xb), np.float32)
    for k, t in TAPS.items():
        for y in range(tile):
            for x in range(xb):
                if y + k < 0:
                    m[x, y, 0, y + k + 3, x] += t
                if y + k >= tile:
                    m[x, y, 1, y + k - tile, x] += t
    return m.reshape(xb * tile, 6 * xb)


def split_dot(mat, val, flip=False):
    hi = val.astype(jnp.bfloat16)
    lo = (val - hi.astype(jnp.float32)).astype(jnp.bfloat16)
    if flip:
        return jnp.dot(hi, mat, preferred_element_type=jnp.float32) + jnp.dot(
            lo, mat, preferred_element_type=jnp.float32
        )
    return jnp.dot(mat, hi, preferred_element_type=jnp.float32) + jnp.dot(
        mat, lo, preferred_element_type=jnp.float32
    )


def pack_kernel(x0, xs, vel, low, high, buf, sem):
    copies = []
    for zb in range(2):
        cp = pltpu.make_async_copy(
            vel.at[:, pl.ds(x0, xs), :, pl.ds(zb * 128, 128)], buf.at[zb], sem.at[zb]
        )
        cp.start()
        copies.append(cp)
    for zb in range(2):
        copies[zb].wait()
        flat = buf.at[zb].reshape(3 * xs * 8, 128)
        for c in range(3):
            for y in range(3):
                low[c, y, :, zb * 128 : (zb + 1) * 128] = flat[
                    pl.ds(c * xs * 8 + y, xs, stride=8), :
                ]
                high[c, y, :, zb * 128 : (zb + 1) * 128] = flat[
                    pl.ds(c * xs * 8 + 5 + y, xs, stride=8), :
                ]


def pack(vel, k):
    comps, nx, ty, nz = vel.shape
    xs = nx // CHUNKS
    out = jax.ShapeDtypeStruct((comps, 3, xs, nz), jnp.float32)
    return pl.pallas_call(
        functools.partial(pack_kernel, k * xs, xs),
        out_shape=(out, out),
        in_specs=[pl.BlockSpec(memory_space=pl.ANY)],
        out_specs=[pl.BlockSpec(memory_space=pltpu.VMEM)] * 2,
        scratch_shapes=[
            pltpu.VMEM((2, comps, xs, ty, 128), jnp.float32),
            pltpu.SemaphoreType.DMA((2,)),
        ],
        compiler_params=pltpu.CompilerParams(vmem_limit_bytes=16 << 20),
        name="pack",
    )(vel)


def ends_kernel(vel, right, left):
    n = vel.shape[1]

    def step(i, carry):
        p_old, p, t_old, t = carry
        return (p, vel[:, i] + R * p, t, vel[:, n - 1 - i] + R * t)

    def steps(b, carry):
        for j in range(8):
            carry = step(b * 8 + j, carry)
        return carry

    carry = (vel[:, 0], vel[:, 0], vel[:, n - 1], vel[:, n - 1])
    for i in range(1, 8):
        carry = step(i, carry)
    p_old, p, t_old, t = lax.fori_loop(1, n // 8, steps, carry)
    right[0] = p_old
    right[1] = p
    left[0] = GAIN * t
    left[1] = GAIN * (t_old + R * vel[:, 0])


def ends(vel):
    comps, nx, ty, nz = vel.shape
    out = jax.ShapeDtypeStruct((2, comps, ty, nz), jnp.float32)
    return pl.pallas_call(
        ends_kernel,
        out_shape=(out, out),
        in_specs=[pl.BlockSpec(memory_space=pltpu.VMEM)],
        out_specs=[pl.BlockSpec(memory_space=pltpu.VMEM)] * 2,
        compiler_params=pltpu.CompilerParams(vmem_limit_bytes=16 << 20),
        name="ends",
    )(vel)


def main_kernel(vel, from_left, from_right, zmat, ymat, adv, deriv):
    comps, n, ty, nz = vel.shape

    def block(b, _):
        rows = pl.ds(b * XB, XB)
        sv = vel[1, rows].reshape(XB * ty, nz) * (-1.0 / 60.0)
        sw = vel[2, rows].reshape(XB * ty, nz) * (-1.0 / 60.0)
        for c in range(comps):
            f = vel[c, rows].reshape(XB * ty, nz)
            gz = split_dot(zmat[...], f, flip=True)
            gy = split_dot(ymat[...], f)
            adv[c, rows] = (sv * gy + sw * gz).reshape(XB, ty, nz)
        return 0

    lax.fori_loop(0, n // XB, block, 0)

    def forward(i, p):
        p = vel[:, i] + R * p
        deriv[:, i] = p
        return p

    p_left = from_left[1]
    p_end = lax.fori_loop(0, n, forward, p_left, unroll=8)
    h_n = from_right[0] + (GAIN * R) * p_end
    h_n1 = from_right[1] + (GAIN * R * R) * p_end

    def emit(i, h2, h1, h_1, h_2):
        g = NEAR * (h1 - h_1) + FAR * (h2 - h_2)
        deriv[:, i] = g
        adv[:, i] = adv[:, i] - vel[0, i][None] * g

    h_a = deriv[:, n - 1] + R * h_n
    h_b = deriv[:, n - 2] + R * h_a

    def backward(k, carry):
        h4, h3, h2, h1 = carry
        i = n - 3 - k
        h = deriv[:, i] + R * h1
        emit(i + 2, h4, h3, h1, h)
        return (h3, h2, h1, h)

    h4, h3, h2, h1 = lax.fori_loop(
        0, n - 2, backward, (h_n1, h_n, h_a, h_b), unroll=6
    )
    h = p_left + R * h1
    emit(1, h4, h3, h1, h)
    h4, h3, h2, h1 = h3, h2, h1, h
    h = from_left[0] + R * h1
    emit(0, h4, h3, h1, h)


def main(vel, from_left, from_right, zmat, ymat):
    out = jax.ShapeDtypeStruct(vel.shape, jnp.float32)
    return pl.pallas_call(
        main_kernel,
        out_shape=(out, out),
        in_specs=[pl.BlockSpec(memory_space=pltpu.VMEM)] * 5,
        out_specs=[pl.BlockSpec(memory_space=pltpu.VMEM)] * 2,
        compiler_params=pltpu.CompilerParams(vmem_limit_bytes=32 << 20),
        name="inner",
    )(vel, from_left, from_right, zmat, ymat)


def final_kernel(adv_in, speed, low, high, hmat, adv):
    comps, xs, ty, nz = adv.shape
    for b in range(xs // XB):
        rows = slice(b * XB, (b + 1) * XB)
        sv = speed[0, rows].reshape(XB * ty, nz) * (1.0 / 60.0)
        for c in range(comps):
            halo = jnp.concatenate(
                [
                    low[c, :, rows].reshape(3 * XB, nz),
                    high[c, :, rows].reshape(3 * XB, nz),
                ],
                axis=0,
            )
            gy = split_dot(hmat[...], halo)
            adv[c, rows] = adv_in[c, rows] - (sv * gy).reshape(XB, ty, nz)


def final(adv, vel, low, high, hmat, k):
    comps, nx, ty, nz = vel.shape
    xs = low.shape[2]
    return pl.pallas_call(
        final_kernel,
        out_shape=jax.ShapeDtypeStruct(vel.shape, jnp.float32),
        grid=(1,),
        in_specs=[
            pl.BlockSpec((comps, xs, ty, nz), lambda i: (0, k, 0, 0)),
            pl.BlockSpec((1, xs, ty, nz), lambda i: (1, k, 0, 0)),
            pl.BlockSpec(memory_space=pltpu.VMEM),
            pl.BlockSpec(memory_space=pltpu.VMEM),
            pl.BlockSpec(memory_space=pltpu.VMEM),
        ],
        out_specs=pl.BlockSpec((comps, xs, ty, nz), lambda i: (0, k, 0, 0)),
        input_output_aliases={0: 0},
        compiler_params=pltpu.CompilerParams(vmem_limit_bytes=32 << 20),
        name="outer",
    )(adv, vel, low, high, hmat)


def shift(x, axis, step):
    count = lax.axis_size(axis)
    return lax.ppermute(x, axis, [(i, (i + step) % count) for i in range(count)])


def on_device(vel):
    comps, nx, ty, nz = vel.shape
    zmat = jnp.asarray(z_matrix(nz), jnp.bfloat16)
    ymat = jnp.asarray(y_matrix(ty, XB), jnp.bfloat16)
    hmat = jnp.asarray(halo_matrix(ty, XB), jnp.bfloat16)
    halos = []
    for k in range(CHUNKS):
        low_rows, high_rows = pack(vel, k)
        halos.append((shift(high_rows, "cross", 1), shift(low_rows, "cross", -1)))
    right, left = ends(vel)
    from_left = shift(right, "line", 1)
    from_right = shift(left, "line", -1)
    adv, deriv = main(vel, from_left, from_right, zmat, ymat)
    for k in range(CHUNKS):
        low, high = halos[k]
        adv = final(adv, vel, low, high, hmat, k)
    return adv, deriv


def solution(mesh):
    spec = P(None, "line", "cross", None)
    return jax.shard_map(
        on_device, mesh=mesh, in_specs=(spec,), out_specs=(spec, spec), check_vma=False
    )
```

```python
import functools

import jax
import jax.numpy as jnp
import numpy as np
from jax import lax
from jax.experimental import pallas as pl
from jax.experimental.pallas import tpu as pltpu
from jax.sharding import PartitionSpec as P

ALPHA = 1.0 / 3.0
ROOT = (-1.0 + np.sqrt(1.0 - 4.0 * ALPHA * ALPHA)) / (2.0 * ALPHA)
KAPPA = -ALPHA / ROOT
NEAR = float(7.0 / 9.0 / KAPPA)
FAR = float(1.0 / 36.0 / KAPPA)
R = float(ROOT)
GAIN = float(1.0 / (1.0 - ROOT * ROOT))
TAPS = {1: 45.0, 2: -9.0, 3: 1.0, -1: -45.0, -2: 9.0, -3: -1.0}
CHUNKS = (32, 64, 32)
XB = 32
LB = 16
EB = 8
LANES = 128


def z_matrix(n):
    m = np.zeros((n, n), np.float32)
    for k, t in TAPS.items():
        for z in range(n):
            m[(z + k) % n, z] += t
    return m


def y_matrix(tile, xb):
    m = np.zeros((tile, tile), np.float32)
    for k, t in TAPS.items():
        for y in range(tile):
            if 0 <= y + k < tile:
                m[y, y + k] += t
    return np.kron(np.eye(xb, dtype=np.float32), m)


def halo_matrix(tile, xb):
    m = np.zeros((xb, tile, 2, 3, xb), np.float32)
    for k, t in TAPS.items():
        for y in range(tile):
            for x in range(xb):
                if y + k < 0:
                    m[x, y, 0, y + k + 3, x] += t
                if y + k >= tile:
                    m[x, y, 1, y + k - tile, x] += t
    return m.reshape(xb * tile, 6 * xb)


def split_dot(mat, val, flip=False):
    hi = val.astype(jnp.bfloat16)
    lo = (val - hi.astype(jnp.float32)).astype(jnp.bfloat16)
    if flip:
        return jnp.dot(hi, mat, preferred_element_type=jnp.float32) + jnp.dot(
            lo, mat, preferred_element_type=jnp.float32
        )
    return jnp.dot(mat, hi, preferred_element_type=jnp.float32) + jnp.dot(
        mat, lo, preferred_element_type=jnp.float32
    )


def pack_rows(held, low, high, row, x0, xs):
    halves, comps, n, tile, lanes = held.shape
    flat = held.reshape(halves * comps * n * tile, lanes)
    for half in range(halves):
        cols = pl.ds(half * lanes, lanes)
        for c in range(comps):
            for y in range(3):
                start = ((half * comps + c) * n + row) * tile + y
                low[c, y, pl.ds(x0, xs), cols] = flat[pl.ds(start, xs, stride=tile)]
                high[c, y, pl.ds(x0, xs), cols] = flat[
                    pl.ds(start + tile - 3, xs, stride=tile)
                ]


def fetch(vel, held, sems, row, count, at):
    copies = []
    for half in range(held.shape[0]):
        copies.append(
            pltpu.make_async_copy(
                vel.at[:, pl.ds(row, count), :, pl.ds(half * LANES, LANES)],
                held.at[half, :, pl.ds(at, count)],
                sems.at[half],
            )
        )
        copies[-1].start()
    return copies


def rows_of(held, c, rows):
    both = [held[half, c, rows] for half in range(held.shape[0])]
    return jnp.concatenate([h.reshape(-1, LANES) for h in both], axis=1)


def put_rows(held, c, rows, val):
    tile = held.shape[3]
    for half in range(held.shape[0]):
        held[half, c, rows] = val[:, half * LANES : (half + 1) * LANES].reshape(
            -1, tile, LANES
        )


def pack_kernel(xs, vel, low, high, buf, sems):
    for cp in fetch(vel, buf, sems, 0, xs, 0):
        cp.wait()
    pack_rows(buf, low, high, 0, 0, xs)


def held_shape(vel, n=None):
    comps, nx, tile, nz = vel.shape
    return pltpu.VMEM((nz // LANES, comps, n or nx, tile, LANES), jnp.float32)


def halo_shape(vel, xs):
    return pltpu.VMEM((vel.shape[0], 3, xs, vel.shape[3]), jnp.float32)


def in_hbm(x):
    return pltpu.with_memory_space_constraint(x, pltpu.HBM)


def pack(vel, xs):
    _, _, _, nz = vel.shape
    return pl.pallas_call(
        functools.partial(pack_kernel, xs),
        out_shape=(halo_shape(vel, xs),) * 2,
        in_specs=[pl.BlockSpec(memory_space=pltpu.HBM)],
        out_specs=[pl.BlockSpec(memory_space=pltpu.VMEM)] * 2,
        scratch_shapes=[
            held_shape(vel, xs),
            pltpu.SemaphoreType.DMA((nz // LANES,)),
        ],
        compiler_params=pltpu.CompilerParams(vmem_limit_bytes=8 << 20),
        name="pack",
    )(in_hbm(vel))


def load_kernel(chunks, vel_in, *refs):
    vel, right, left = refs[:3]
    sends, sems = refs[3:-1], refs[-1]
    n = vel.shape[2]
    copies = [
        fetch(vel_in, vel, sems.at[b], b * LB, LB, b * LB) for b in range(n // LB)
    ]
    where = []
    x0 = 0
    for k, xs in enumerate(chunks):
        where += [(k, x0)] * (xs // LB)
        x0 += xs
    p_old = p = t = t_one = None
    power = 1.0
    for b in range(n // LB):
        for cp in copies[b]:
            cp.wait()
        k, x0 = where[b]
        if k > 0:
            pack_rows(
                vel, sends[2 * k - 2], sends[2 * k - 1], b * LB, b * LB - x0, LB
            )
        for i in range(b * LB, (b + 1) * LB):
            f = vel[:, :, i]
            if i == 0:
                p, t = f, f
            else:
                p_old, p = p, f + R * p
                t = t + float(np.float32(power)) * f
            power *= R
    right[0] = p_old
    right[1] = p
    first = vel[:, :, 0]
    left[0] = GAIN * t
    left[1] = GAIN * ((t - first) * (1.0 / R) + R * first)


def load(vel, chunks):
    comps, nx, tile, nz = vel.shape
    edge = pltpu.VMEM((2, nz // LANES, comps, tile, LANES), jnp.float32)
    outs = [held_shape(vel), edge, edge]
    for xs in chunks[1:]:
        outs += [halo_shape(vel, xs)] * 2
    return pl.pallas_call(
        functools.partial(load_kernel, chunks),
        out_shape=tuple(outs),
        in_specs=[pl.BlockSpec(memory_space=pltpu.HBM)],
        out_specs=[pl.BlockSpec(memory_space=pltpu.VMEM)] * len(outs),
        scratch_shapes=[pltpu.SemaphoreType.DMA((nx // LB, nz // LANES))],
        compiler_params=pltpu.CompilerParams(vmem_limit_bytes=16 << 20),
        name="load",
    )(in_hbm(vel))


def inner_kernel(vel, zmat, ymat, adv):
    _, comps, n, _, _ = vel.shape

    def block(b, _):
        rows = pl.ds(b * XB, XB)
        sv = rows_of(vel, 1, rows) * (-1.0 / 60.0)
        sw = rows_of(vel, 2, rows) * (-1.0 / 60.0)
        for c in range(comps):
            f = rows_of(vel, c, rows)
            gz = split_dot(zmat[...], f, flip=True)
            gy = split_dot(ymat[...], f)
            put_rows(adv, c, rows, sv * gy + sw * gz)
        return 0

    lax.fori_loop(0, n // XB, block, 0)


def inner(vel, zmat, ymat):
    return pl.pallas_call(
        inner_kernel,
        out_shape=pltpu.VMEM(vel.shape, jnp.float32),
        in_specs=[pl.BlockSpec(memory_space=pltpu.VMEM)] * 3,
        out_specs=pl.BlockSpec(memory_space=pltpu.VMEM),
        compiler_params=pltpu.CompilerParams(vmem_limit_bytes=8 << 20),
        name="inner",
    )(vel, zmat, ymat)


def along_kernel(vel, from_left, from_right, adv_in, adv, deriv_out, deriv, sems):
    halves, _, n, _, _ = vel.shape

    def forward(b, p):
        for j in range(EB):
            i = b * EB + j
            p = vel[:, :, i] + R * p
            deriv[:, :, i] = p
        return p

    p_left = from_left[1]
    p_end = lax.fori_loop(0, n // EB, forward, p_left)
    h_n = from_right[0] + (GAIN * R) * p_end
    h_n1 = from_right[1] + (GAIN * R * R) * p_end
    h_a = deriv[:, :, n - 1] + R * h_n
    h_b = deriv[:, :, n - 2] + R * h_a

    def copy_out(b):
        rows = pl.ds(b * EB, EB)
        return [
            pltpu.make_async_copy(
                deriv.at[half, :, rows],
                deriv_out.at[:, rows, :, pl.ds(half * LANES, LANES)],
                sems.at[b, half],
            )
            for half in range(halves)
        ]

    def backward(b, carry, last=False):
        h4, h3, h2, h1 = carry
        for j in range(EB):
            i = b * EB + EB - 1 - j
            if last and i < 2:
                p = p_left if i == 1 else from_left[0]
            else:
                p = deriv[:, :, i - 2]
            h = p + R * h1
            g = NEAR * (h3 - h1) + FAR * (h4 - h)
            deriv[:, :, i] = g
            adv[:, :, i] = adv_in[:, :, i] - vel[:, 0, i][:, None] * g
            h4, h3, h2, h1 = h3, h2, h1, h
        for cp in copy_out(b):
            cp.start()
        return (h4, h3, h2, h1)

    blocks = n // EB
    carry = lax.fori_loop(
        0, blocks - 1, lambda k, c: backward(blocks - 1 - k, c), (h_n1, h_n, h_a, h_b)
    )
    backward(0, carry, last=True)
    for b in range(blocks):
        for cp in copy_out(b):
            cp.wait()


def along(vel, from_left, from_right, adv):
    halves, comps, nx, tile, lanes = vel.shape
    return pl.pallas_call(
        along_kernel,
        out_shape=(pltpu.VMEM(vel.shape, jnp.float32), jax.ShapeDtypeStruct((comps, nx, tile, halves * lanes), jnp.float32)),
        in_specs=[pl.BlockSpec(memory_space=pltpu.VMEM)] * 4,
        out_specs=[
            pl.BlockSpec(memory_space=pltpu.VMEM),
            pl.BlockSpec(memory_space=pl.ANY),
        ],
        scratch_shapes=[
            pltpu.VMEM(vel.shape, jnp.float32),
            pltpu.SemaphoreType.DMA((nx // EB, halves)),
        ],
        input_output_aliases={3: 0},
        compiler_params=pltpu.CompilerParams(vmem_limit_bytes=16 << 20),
        name="along",
    )(vel, from_left, from_right, adv)


def outer_kernel(x0, *refs):
    vel, adv_in, low, high, hmat = refs[:5]
    adv_out, adv, sems = refs[-3:]
    halves, comps, xs, _, lanes = adv.shape
    copies = []
    for b in range(xs // XB):
        here = pl.ds(b * XB, XB)
        rows = pl.ds(x0 + b * XB, XB)
        sv = rows_of(vel, 1, rows) * (1.0 / 60.0)
        for c in range(comps):
            halo = jnp.concatenate(
                [
                    low[c, :, here].reshape(-1, halves * lanes),
                    high[c, :, here].reshape(-1, halves * lanes),
                ],
                axis=0,
            )
            gy = split_dot(hmat[...], halo)
            put_rows(adv, c, here, rows_of(adv_in, c, rows) - sv * gy)
            for half in range(halves):
                copies.append(
                    pltpu.make_async_copy(
                        adv.at[half, c, here],
                        adv_out.at[c, rows, :, pl.ds(half * LANES, LANES)],
                        sems.at[b * comps + c, half],
                    )
                )
                copies[-1].start()
    for cp in copies:
        cp.wait()


def outer(vel, adv, low, high, hmat, x0, out):
    halves, comps, nx, tile, lanes = vel.shape
    xs = low.shape[2]
    args = [vel, adv, low, high, hmat]
    specs = [pl.BlockSpec(memory_space=pltpu.VMEM)] * 5
    alias = {}
    if out is not None:
        args.append(out)
        specs.append(pl.BlockSpec(memory_space=pl.ANY))
        alias = {5: 0}
    return pl.pallas_call(
        functools.partial(outer_kernel, x0),
        out_shape=jax.ShapeDtypeStruct((comps, nx, tile, halves * lanes), jnp.float32),
        in_specs=specs,
        out_specs=pl.BlockSpec(memory_space=pl.ANY),
        scratch_shapes=[
            pltpu.VMEM((halves, comps, xs, tile, lanes), jnp.float32),
            pltpu.SemaphoreType.DMA((comps * (xs // XB), halves)),
        ],
        input_output_aliases=alias,
        compiler_params=pltpu.CompilerParams(vmem_limit_bytes=8 << 20),
        name="outer",
    )(*args)


def shift(x, axis, step):
    count = lax.axis_size(axis)
    return lax.ppermute(x, axis, [(i, (i + step) % count) for i in range(count)])


def on_device(vel):
    _, _, tile, nz = vel.shape
    zmat = jnp.asarray(z_matrix(nz), jnp.bfloat16)
    ymat = jnp.asarray(y_matrix(tile, XB), jnp.bfloat16)
    hmat = jnp.asarray(halo_matrix(tile, XB), jnp.bfloat16)
    sends = list(pack(vel, CHUNKS[0]))
    held, right, left, *rest = load(vel, CHUNKS)
    sends += rest
    halos = []
    for k in range(len(CHUNKS)):
        low_rows, high_rows = sends[2 * k : 2 * k + 2]
        halos.append((shift(high_rows, "cross", 1), shift(low_rows, "cross", -1)))
    from_left = shift(right, "line", 1)
    from_right = shift(left, "line", -1)
    adv = inner(held, zmat, ymat)
    adv, deriv = along(held, from_left, from_right, adv)
    out = None
    x0 = 0
    for xs, (low, high) in zip(CHUNKS, halos):
        out = outer(held, adv, low, high, hmat, x0, out)
        x0 += xs
    return out, deriv


def solution(mesh):
    spec = P(None, "line", "cross", None)
    return jax.shard_map(
        on_device,
        mesh=mesh,
        in_specs=(spec,),
        out_specs=(spec, spec),
        check_vma=False,
    )
```

```python
import functools

import jax
import jax.numpy as jnp
import numpy as np
from jax import lax
from jax.experimental import pallas as pl
from jax.experimental.pallas import tpu as pltpu
from jax.sharding import PartitionSpec as P

ALPHA = 1.0 / 3.0
ROOT = (-1.0 + np.sqrt(1.0 - 4.0 * ALPHA * ALPHA)) / (2.0 * ALPHA)
KAPPA = -ALPHA / ROOT
NEAR = float(7.0 / 9.0 / KAPPA)
FAR = float(1.0 / 36.0 / KAPPA)
R = float(ROOT)
GAIN = float(1.0 / (1.0 - ROOT * ROOT))
TAPS = {1: 45.0, 2: -9.0, 3: 1.0, -1: -45.0, -2: 9.0, -3: -1.0}
CHUNKS = (32, 64, 32)
XB = 32
LB = 16
EB = 8
LANES = 128


def z_matrix(n):
    m = np.zeros((n, n), np.float32)
    for k, t in TAPS.items():
        for z in range(n):
            m[(z + k) % n, z] += t
    return m


def y_matrix(tile, xb):
    m = np.zeros((tile, tile), np.float32)
    for k, t in TAPS.items():
        for y in range(tile):
            if 0 <= y + k < tile:
                m[y, y + k] += t
    return np.kron(np.eye(xb, dtype=np.float32), m)


def halo_matrices(tile, xb):
    m = np.zeros((2, xb, tile, 3, xb), np.float32)
    for k, t in TAPS.items():
        for y in range(tile):
            for x in range(xb):
                if y + k < 0:
                    m[0, x, y, y + k + 3, x] += t
                if y + k >= tile:
                    m[1, x, y, y + k - tile, x] += t
    return m.reshape(2, xb * tile, 3 * xb)


def parity():
    return lax.rem(lax.axis_index("cross"), 2)


def split_dot(mat, val, flip=False):
    hi = val.astype(jnp.bfloat16)
    lo = (val - hi.astype(jnp.float32)).astype(jnp.bfloat16)
    if flip:
        return jnp.dot(hi, mat, preferred_element_type=jnp.float32) + jnp.dot(
            lo, mat, preferred_element_type=jnp.float32
        )
    return jnp.dot(mat, hi, preferred_element_type=jnp.float32) + jnp.dot(
        mat, lo, preferred_element_type=jnp.float32
    )


def pack_rows(held, out, first, row, x0, xs):
    halves, comps, n, tile, lanes = held.shape
    flat = held.reshape(halves * comps * n * tile, lanes)
    for half in range(halves):
        cols = pl.ds(half * lanes, lanes)
        for c in range(comps):
            for y in range(3):
                start = ((half * comps + c) * n + row) * tile + y
                out[c, y, pl.ds(x0, xs), cols] = flat[
                    pl.ds(start + first, xs, stride=tile)
                ]


def fetch(vel, held, sems, row, count, at):
    copies = []
    for half in range(held.shape[0]):
        copies.append(
            pltpu.make_async_copy(
                vel.at[:, pl.ds(row, count), :, pl.ds(half * LANES, LANES)],
                held.at[half, :, pl.ds(at, count)],
                sems.at[half],
            )
        )
        copies[-1].start()
    return copies


def rows_of(held, c, rows):
    both = [held[half, c, rows] for half in range(held.shape[0])]
    return jnp.concatenate([h.reshape(-1, LANES) for h in both], axis=1)


def put_rows(held, c, rows, val):
    tile = held.shape[3]
    for half in range(held.shape[0]):
        held[half, c, rows] = val[:, half * LANES : (half + 1) * LANES].reshape(
            -1, tile, LANES
        )


def pack_kernel(xs, vel, cross, buf, sems):
    copies = fetch(vel, buf, sems, 0, xs, 0)
    first = parity() * (buf.shape[3] - 3)
    for cp in copies:
        cp.wait()
    pack_rows(buf, cross, first, 0, 0, xs)


def held_shape(vel, n=None):
    comps, nx, tile, nz = vel.shape
    return pltpu.VMEM((nz // LANES, comps, n or nx, tile, LANES), jnp.float32)


def halo_shape(vel, xs):
    return pltpu.VMEM((vel.shape[0], 3, xs, vel.shape[3]), jnp.float32)


def in_hbm(x):
    return pltpu.with_memory_space_constraint(x, pltpu.HBM)


def pack(vel, xs):
    _, _, _, nz = vel.shape
    return pl.pallas_call(
        functools.partial(pack_kernel, xs),
        out_shape=halo_shape(vel, xs),
        in_specs=[pl.BlockSpec(memory_space=pltpu.HBM)],
        out_specs=pl.BlockSpec(memory_space=pltpu.VMEM),
        scratch_shapes=[
            held_shape(vel, xs),
            pltpu.SemaphoreType.DMA((nz // LANES,)),
        ],
        compiler_params=pltpu.CompilerParams(vmem_limit_bytes=8 << 20),
        name="pack",
    )(in_hbm(vel))


def load_kernel(chunks, vel_in, *refs):
    vel, right, left, chip = refs[:4]
    cross, sems = refs[4:-1], refs[-1]
    n, tile = vel.shape[2:4]
    to_cross = parity() * (tile - 3)
    to_chip = tile - 3 - to_cross
    copies = [
        fetch(vel_in, vel, sems.at[b], b * LB, LB, b * LB) for b in range(n // LB)
    ]
    where = []
    x0 = 0
    for k, xs in enumerate(chunks):
        where += [(k, x0)] * (xs // LB)
        x0 += xs
    p_old = p = t = t_one = None
    power = 1.0
    for b in range(n // LB):
        for cp in copies[b]:
            cp.wait()
        k, x0 = where[b]
        pack_rows(vel, chip, to_chip, b * LB, b * LB, LB)
        if k > 0:
            pack_rows(vel, cross[k - 1], to_cross, b * LB, b * LB - x0, LB)
        for i in range(b * LB, (b + 1) * LB):
            f = vel[:, :, i]
            if i == 0:
                p, t = f, f
            else:
                p_old, p = p, f + R * p
                t = t + float(np.float32(power)) * f
            power *= R
    right[0] = p_old
    right[1] = p
    first = vel[:, :, 0]
    left[0] = GAIN * t
    left[1] = GAIN * ((t - first) * (1.0 / R) + R * first)


def load(vel, chunks):
    comps, nx, tile, nz = vel.shape
    edge = pltpu.VMEM((2, nz // LANES, comps, tile, LANES), jnp.float32)
    outs = [held_shape(vel), edge, edge, halo_shape(vel, nx)]
    outs += [halo_shape(vel, xs) for xs in chunks[1:]]
    return pl.pallas_call(
        functools.partial(load_kernel, chunks),
        out_shape=tuple(outs),
        in_specs=[pl.BlockSpec(memory_space=pltpu.HBM)],
        out_specs=[pl.BlockSpec(memory_space=pltpu.VMEM)] * len(outs),
        scratch_shapes=[pltpu.SemaphoreType.DMA((nx // LB, nz // LANES))],
        compiler_params=pltpu.CompilerParams(vmem_limit_bytes=16 << 20),
        name="load",
    )(in_hbm(vel))


def inner_kernel(vel, chip, zmat, ymat, hmat, adv):
    halves, comps, n, _, lanes = vel.shape
    side = 1 - parity()

    def block(b, _):
        rows = pl.ds(b * XB, XB)
        sv = rows_of(vel, 1, rows) * (-1.0 / 60.0)
        sw = rows_of(vel, 2, rows) * (-1.0 / 60.0)
        for c in range(comps):
            f = rows_of(vel, c, rows)
            gz = split_dot(zmat[...], f, flip=True)
            gy = split_dot(ymat[...], f)
            halo = chip[c, :, rows].reshape(-1, halves * lanes)
            gy = gy + split_dot(hmat[side], halo)
            put_rows(adv, c, rows, sv * gy + sw * gz)
        return 0

    lax.fori_loop(0, n // XB, block, 0)


def inner(vel, chip, zmat, ymat, hmat):
    return pl.pallas_call(
        inner_kernel,
        out_shape=pltpu.VMEM(vel.shape, jnp.float32),
        in_specs=[pl.BlockSpec(memory_space=pltpu.VMEM)] * 5,
        out_specs=pl.BlockSpec(memory_space=pltpu.VMEM),
        compiler_params=pltpu.CompilerParams(vmem_limit_bytes=8 << 20),
        name="inner",
    )(vel, chip, zmat, ymat, hmat)


def along_kernel(vel, from_left, from_right, adv_in, adv, deriv_out, deriv, sems):
    halves, _, n, _, _ = vel.shape

    def forward(b, p):
        for j in range(EB):
            i = b * EB + j
            p = vel[:, :, i] + R * p
            deriv[:, :, i] = p
        return p

    p_left = from_left[1]
    p_end = lax.fori_loop(0, n // EB, forward, p_left)
    h_n = from_right[0] + (GAIN * R) * p_end
    h_n1 = from_right[1] + (GAIN * R * R) * p_end
    h_a = deriv[:, :, n - 1] + R * h_n
    h_b = deriv[:, :, n - 2] + R * h_a

    def copy_out(b):
        rows = pl.ds(b * EB, EB)
        return [
            pltpu.make_async_copy(
                deriv.at[half, :, rows],
                deriv_out.at[:, rows, :, pl.ds(half * LANES, LANES)],
                sems.at[b, half],
            )
            for half in range(halves)
        ]

    def backward(b, carry, last=False):
        h4, h3, h2, h1 = carry
        for j in range(EB):
            i = b * EB + EB - 1 - j
            if last and i < 2:
                p = p_left if i == 1 else from_left[0]
            else:
                p = deriv[:, :, i - 2]
            h = p + R * h1
            g = NEAR * (h3 - h1) + FAR * (h4 - h)
            deriv[:, :, i] = g
            adv[:, :, i] = adv_in[:, :, i] - vel[:, 0, i][:, None] * g
            h4, h3, h2, h1 = h3, h2, h1, h
        for cp in copy_out(b):
            cp.start()
        return (h4, h3, h2, h1)

    blocks = n // EB
    carry = lax.fori_loop(
        0, blocks - 1, lambda k, c: backward(blocks - 1 - k, c), (h_n1, h_n, h_a, h_b)
    )
    backward(0, carry, last=True)
    for b in range(blocks):
        for cp in copy_out(b):
            cp.wait()


def along(vel, from_left, from_right, adv):
    halves, comps, nx, tile, lanes = vel.shape
    return pl.pallas_call(
        along_kernel,
        out_shape=(pltpu.VMEM(vel.shape, jnp.float32), jax.ShapeDtypeStruct((comps, nx, tile, halves * lanes), jnp.float32)),
        in_specs=[pl.BlockSpec(memory_space=pltpu.VMEM)] * 4,
        out_specs=[
            pl.BlockSpec(memory_space=pltpu.VMEM),
            pl.BlockSpec(memory_space=pl.ANY),
        ],
        scratch_shapes=[
            pltpu.VMEM(vel.shape, jnp.float32),
            pltpu.SemaphoreType.DMA((nx // EB, halves)),
        ],
        input_output_aliases={3: 0},
        compiler_params=pltpu.CompilerParams(vmem_limit_bytes=16 << 20),
        name="along",
    )(vel, from_left, from_right, adv)


def outer_kernel(x0, *refs):
    vel, adv_in, cross, hmat = refs[:4]
    adv_out, adv, sems = refs[-3:]
    halves, comps, xs, _, lanes = adv.shape
    side = parity()
    copies = []
    for b in range(xs // XB):
        here = pl.ds(b * XB, XB)
        rows = pl.ds(x0 + b * XB, XB)
        sv = rows_of(vel, 1, rows) * (1.0 / 60.0)
        for c in range(comps):
            halo = cross[c, :, here].reshape(-1, halves * lanes)
            gy = split_dot(hmat[side], halo)
            put_rows(adv, c, here, rows_of(adv_in, c, rows) - sv * gy)
            for half in range(halves):
                copies.append(
                    pltpu.make_async_copy(
                        adv.at[half, c, here],
                        adv_out.at[c, rows, :, pl.ds(half * LANES, LANES)],
                        sems.at[b * comps + c, half],
                    )
                )
                copies[-1].start()
    for cp in copies:
        cp.wait()


def outer(vel, adv, cross, hmat, x0, out):
    halves, comps, nx, tile, lanes = vel.shape
    xs = cross.shape[2]
    args = [vel, adv, cross, hmat]
    specs = [pl.BlockSpec(memory_space=pltpu.VMEM)] * 4
    alias = {}
    if out is not None:
        args.append(out)
        specs.append(pl.BlockSpec(memory_space=pl.ANY))
        alias = {4: 0}
    return pl.pallas_call(
        functools.partial(outer_kernel, x0),
        out_shape=jax.ShapeDtypeStruct((comps, nx, tile, halves * lanes), jnp.float32),
        in_specs=specs,
        out_specs=pl.BlockSpec(memory_space=pl.ANY),
        scratch_shapes=[
            pltpu.VMEM((halves, comps, xs, tile, lanes), jnp.float32),
            pltpu.SemaphoreType.DMA((comps * (xs // XB), halves)),
        ],
        input_output_aliases=alias,
        compiler_params=pltpu.CompilerParams(vmem_limit_bytes=8 << 20),
        name="outer",
    )(*args)


def shift(x, axis, step):
    count = lax.axis_size(axis)
    return lax.ppermute(x, axis, [(i, (i + step) % count) for i in range(count)])


def swap(x, axis, step):
    count = lax.axis_size(axis)
    pairs = []
    for i in range(0, count, 2):
        j = (i + step) % count
        pairs += [(i, j), (j, i)]
    return lax.ppermute(x, axis, pairs)


def on_device(vel):
    _, _, tile, nz = vel.shape
    zmat = jnp.asarray(z_matrix(nz), jnp.bfloat16)
    ymat = jnp.asarray(y_matrix(tile, XB), jnp.bfloat16)
    hmat = jnp.asarray(halo_matrices(tile, XB), jnp.bfloat16)
    first = pack(vel, CHUNKS[0])
    held, right, left, chip, *rest = load(vel, CHUNKS)
    halos = [swap(x, "cross", -1) for x in [first] + rest]
    chip = swap(chip, "cross", 1)
    from_left = shift(right, "line", 1)
    from_right = shift(left, "line", -1)
    adv = inner(held, chip, zmat, ymat, hmat)
    adv, deriv = along(held, from_left, from_right, adv)
    out = None
    x0 = 0
    for xs, halo in zip(CHUNKS, halos):
        out = outer(held, adv, halo, hmat, x0, out)
        x0 += xs
    return out, deriv


def solution(mesh):
    spec = P(None, "line", "cross", None)
    return jax.shard_map(
        on_device,
        mesh=mesh,
        in_specs=(spec,),
        out_specs=(spec, spec),
        check_vma=False,
    )
```

```python
import functools

import jax
import jax.numpy as jnp
import numpy as np
from jax import lax
from jax.experimental import pallas as pl
from jax.experimental.pallas import tpu as pltpu
from jax.sharding import PartitionSpec as P

ALPHA = 1.0 / 3.0
ROOT = (-1.0 + np.sqrt(1.0 - 4.0 * ALPHA * ALPHA)) / (2.0 * ALPHA)
KAPPA = -ALPHA / ROOT
NEAR = float(7.0 / 9.0 / KAPPA)
FAR = float(1.0 / 36.0 / KAPPA)
R = float(ROOT)
GAIN = float(1.0 / (1.0 - ROOT * ROOT))
TAPS = {1: 45.0, 2: -9.0, 3: 1.0, -1: -45.0, -2: 9.0, -3: -1.0}
CHUNKS = (96, 32)
XB = 32
LB = 16
EB = 8
LANES = 128


def z_matrix(n):
    m = np.zeros((n, n), np.float32)
    for k, t in TAPS.items():
        for z in range(n):
            m[(z + k) % n, z] += t
    return m


def y_matrix(tile, xb):
    m = np.zeros((tile, tile), np.float32)
    for k, t in TAPS.items():
        for y in range(tile):
            if 0 <= y + k < tile:
                m[y, y + k] += t
    return np.kron(np.eye(xb, dtype=np.float32), m)


def halo_matrices(tile, xb):
    m = np.zeros((2, xb, tile, 3, xb), np.float32)
    for k, t in TAPS.items():
        for y in range(tile):
            for x in range(xb):
                if y + k < 0:
                    m[0, x, y, y + k + 3, x] += t
                if y + k >= tile:
                    m[1, x, y, y + k - tile, x] += t
    return m.reshape(2, xb * tile, 3 * xb)


def parity():
    return lax.rem(lax.axis_index("cross"), 2)


def split_dot(mat, val, flip=False):
    hi = val.astype(jnp.bfloat16)
    lo = (val - hi.astype(jnp.float32)).astype(jnp.bfloat16)
    if flip:
        return jnp.dot(hi, mat, preferred_element_type=jnp.float32) + jnp.dot(
            lo, mat, preferred_element_type=jnp.float32
        )
    return jnp.dot(mat, hi, preferred_element_type=jnp.float32) + jnp.dot(
        mat, lo, preferred_element_type=jnp.float32
    )


def pack_rows(held, out, first, row, x0, xs):
    halves, comps, n, tile, lanes = held.shape
    flat = held.reshape(halves * comps * n * tile, lanes)
    for half in range(halves):
        cols = pl.ds(half * lanes, lanes)
        for c in range(comps):
            for y in range(3):
                start = ((half * comps + c) * n + row) * tile + y
                out[c, y, pl.ds(x0, xs), cols] = flat[
                    pl.ds(start + first, xs, stride=tile)
                ]


def fetch(vel, held, sems, row, count, at):
    copies = []
    for half in range(held.shape[0]):
        copies.append(
            pltpu.make_async_copy(
                vel.at[:, pl.ds(row, count), :, pl.ds(half * LANES, LANES)],
                held.at[half, :, pl.ds(at, count)],
                sems.at[half],
            )
        )
        copies[-1].start()
    return copies


def rows_of(held, c, rows):
    both = [held[half, c, rows] for half in range(held.shape[0])]
    return jnp.concatenate([h.reshape(-1, LANES) for h in both], axis=1)


def put_rows(held, c, rows, val):
    tile = held.shape[3]
    for half in range(held.shape[0]):
        held[half, c, rows] = val[:, half * LANES : (half + 1) * LANES].reshape(
            -1, tile, LANES
        )


def held_shape(vel, n=None):
    comps, nx, tile, nz = vel.shape
    return pltpu.VMEM((nz // LANES, comps, n or nx, tile, LANES), jnp.float32)


def halo_shape(vel, xs):
    return pltpu.VMEM((vel.shape[0], 3, xs, vel.shape[3]), jnp.float32)


def in_hbm(x):
    return pltpu.with_memory_space_constraint(x, pltpu.HBM)


def load_kernel(chunks, vel_in, *refs):
    vel, right, left, chip = refs[:4]
    cross, sems = refs[4:-1], refs[-1]
    n, tile = vel.shape[2:4]
    to_cross = parity() * (tile - 3)
    to_chip = tile - 3 - to_cross
    copies = [
        fetch(vel_in, vel, sems.at[b], b * LB, LB, b * LB) for b in range(n // LB)
    ]
    where = []
    x0 = 0
    for k, xs in enumerate(chunks):
        where += [(k, x0)] * (xs // LB)
        x0 += xs
    p_old = p = t = t_one = None
    power = 1.0
    for b in range(n // LB):
        for cp in copies[b]:
            cp.wait()
        k, x0 = where[b]
        pack_rows(vel, chip, to_chip, b * LB, b * LB, LB)
        pack_rows(vel, cross[k], to_cross, b * LB, b * LB - x0, LB)
        for i in range(b * LB, (b + 1) * LB):
            f = vel[:, :, i]
            if i == 0:
                p, t = f, f
            else:
                p_old, p = p, f + R * p
                t = t + float(np.float32(power)) * f
            power *= R
    right[0] = p_old
    right[1] = p
    first = vel[:, :, 0]
    left[0] = GAIN * t
    left[1] = GAIN * ((t - first) * (1.0 / R) + R * first)


def load(vel, chunks):
    comps, nx, tile, nz = vel.shape
    edge = pltpu.VMEM((2, nz // LANES, comps, tile, LANES), jnp.float32)
    outs = [held_shape(vel), edge, edge, halo_shape(vel, nx)]
    outs += [halo_shape(vel, xs) for xs in chunks]
    return pl.pallas_call(
        functools.partial(load_kernel, chunks),
        out_shape=tuple(outs),
        in_specs=[pl.BlockSpec(memory_space=pltpu.HBM)],
        out_specs=[pl.BlockSpec(memory_space=pltpu.VMEM)] * len(outs),
        scratch_shapes=[pltpu.SemaphoreType.DMA((nx // LB, nz // LANES))],
        compiler_params=pltpu.CompilerParams(vmem_limit_bytes=16 << 20),
        name="load",
    )(in_hbm(vel))


def inner_kernel(vel, chip, zmat, ymat, hmat, adv):
    halves, comps, n, _, lanes = vel.shape
    side = 1 - parity()

    def block(b, _):
        rows = pl.ds(b * XB, XB)
        sv = rows_of(vel, 1, rows) * (-1.0 / 60.0)
        sw = rows_of(vel, 2, rows) * (-1.0 / 60.0)
        for c in range(comps):
            f = rows_of(vel, c, rows)
            gz = split_dot(zmat[...], f, flip=True)
            gy = split_dot(ymat[...], f)
            halo = chip[c, :, rows].reshape(-1, halves * lanes)
            gy = gy + split_dot(hmat[side], halo)
            put_rows(adv, c, rows, sv * gy + sw * gz)
        return 0

    lax.fori_loop(0, n // XB, block, 0)


def inner(vel, chip, zmat, ymat, hmat):
    return pl.pallas_call(
        inner_kernel,
        out_shape=pltpu.VMEM(vel.shape, jnp.float32),
        in_specs=[pl.BlockSpec(memory_space=pltpu.VMEM)] * 5,
        out_specs=pl.BlockSpec(memory_space=pltpu.VMEM),
        compiler_params=pltpu.CompilerParams(vmem_limit_bytes=8 << 20),
        name="inner",
    )(vel, chip, zmat, ymat, hmat)


def along_kernel(vel, from_left, from_right, adv_in, adv, deriv_out, deriv, sems):
    halves, _, n, _, _ = vel.shape

    def forward(b, p):
        for j in range(EB):
            i = b * EB + j
            p = vel[:, :, i] + R * p
            deriv[:, :, i] = p
        return p

    p_left = from_left[1]
    p_end = lax.fori_loop(0, n // EB, forward, p_left)
    h_n = from_right[0] + (GAIN * R) * p_end
    h_n1 = from_right[1] + (GAIN * R * R) * p_end
    h_a = deriv[:, :, n - 1] + R * h_n
    h_b = deriv[:, :, n - 2] + R * h_a

    def copy_out(b):
        rows = pl.ds(b * EB, EB)
        return [
            pltpu.make_async_copy(
                deriv.at[half, :, rows],
                deriv_out.at[:, rows, :, pl.ds(half * LANES, LANES)],
                sems.at[b, half],
            )
            for half in range(halves)
        ]

    def backward(b, carry, last=False):
        h4, h3, h2, h1 = carry
        for j in range(EB):
            i = b * EB + EB - 1 - j
            if last and i < 2:
                p = p_left if i == 1 else from_left[0]
            else:
                p = deriv[:, :, i - 2]
            h = p + R * h1
            g = NEAR * (h3 - h1) + FAR * (h4 - h)
            deriv[:, :, i] = g
            adv[:, :, i] = adv_in[:, :, i] - vel[:, 0, i][:, None] * g
            h4, h3, h2, h1 = h3, h2, h1, h
        for cp in copy_out(b):
            cp.start()
        return (h4, h3, h2, h1)

    blocks = n // EB
    carry = lax.fori_loop(
        0, blocks - 1, lambda k, c: backward(blocks - 1 - k, c), (h_n1, h_n, h_a, h_b)
    )
    backward(0, carry, last=True)
    for b in range(blocks):
        for cp in copy_out(b):
            cp.wait()


def along(vel, from_left, from_right, adv):
    halves, comps, nx, tile, lanes = vel.shape
    return pl.pallas_call(
        along_kernel,
        out_shape=(pltpu.VMEM(vel.shape, jnp.float32), jax.ShapeDtypeStruct((comps, nx, tile, halves * lanes), jnp.float32)),
        in_specs=[pl.BlockSpec(memory_space=pltpu.VMEM)] * 4,
        out_specs=[
            pl.BlockSpec(memory_space=pltpu.VMEM),
            pl.BlockSpec(memory_space=pl.ANY),
        ],
        scratch_shapes=[
            pltpu.VMEM(vel.shape, jnp.float32),
            pltpu.SemaphoreType.DMA((nx // EB, halves)),
        ],
        input_output_aliases={3: 0},
        compiler_params=pltpu.CompilerParams(vmem_limit_bytes=16 << 20),
        name="along",
    )(vel, from_left, from_right, adv)


def outer_kernel(x0, *refs):
    vel, adv_in, cross, hmat = refs[:4]
    adv_out, adv, sems = refs[-3:]
    halves, comps, xs, _, lanes = adv.shape
    side = parity()
    copies = []
    for b in range(xs // XB):
        here = pl.ds(b * XB, XB)
        rows = pl.ds(x0 + b * XB, XB)
        sv = rows_of(vel, 1, rows) * (1.0 / 60.0)
        for c in range(comps):
            halo = cross[c, :, here].reshape(-1, halves * lanes)
            gy = split_dot(hmat[side], halo)
            put_rows(adv, c, here, rows_of(adv_in, c, rows) - sv * gy)
            for half in range(halves):
                copies.append(
                    pltpu.make_async_copy(
                        adv.at[half, c, here],
                        adv_out.at[c, rows, :, pl.ds(half * LANES, LANES)],
                        sems.at[b * comps + c, half],
                    )
                )
                copies[-1].start()
    for cp in copies:
        cp.wait()


def outer(vel, adv, cross, hmat, x0, out):
    halves, comps, nx, tile, lanes = vel.shape
    xs = cross.shape[2]
    args = [vel, adv, cross, hmat]
    specs = [pl.BlockSpec(memory_space=pltpu.VMEM)] * 4
    alias = {}
    if out is not None:
        args.append(out)
        specs.append(pl.BlockSpec(memory_space=pl.ANY))
        alias = {4: 0}
    return pl.pallas_call(
        functools.partial(outer_kernel, x0),
        out_shape=jax.ShapeDtypeStruct((comps, nx, tile, halves * lanes), jnp.float32),
        in_specs=specs,
        out_specs=pl.BlockSpec(memory_space=pl.ANY),
        scratch_shapes=[
            pltpu.VMEM((halves, comps, xs, tile, lanes), jnp.float32),
            pltpu.SemaphoreType.DMA((comps * (xs // XB), halves)),
        ],
        input_output_aliases=alias,
        compiler_params=pltpu.CompilerParams(vmem_limit_bytes=8 << 20),
        name="outer",
    )(*args)


def shift(x, axis, step):
    count = lax.axis_size(axis)
    return lax.ppermute(x, axis, [(i, (i + step) % count) for i in range(count)])


def swap(x, axis, step):
    count = lax.axis_size(axis)
    pairs = []
    for i in range(0, count, 2):
        j = (i + step) % count
        pairs += [(i, j), (j, i)]
    return lax.ppermute(x, axis, pairs)


def on_device(vel):
    _, _, tile, nz = vel.shape
    zmat = jnp.asarray(z_matrix(nz), jnp.bfloat16)
    ymat = jnp.asarray(y_matrix(tile, XB), jnp.bfloat16)
    hmat = jnp.asarray(halo_matrices(tile, XB), jnp.bfloat16)
    held, right, left, chip, *cross = load(vel, CHUNKS)
    halos = [swap(x, "cross", -1) for x in cross]
    chip = swap(chip, "cross", 1)
    from_left = shift(right, "line", 1)
    from_right = shift(left, "line", -1)
    adv = inner(held, chip, zmat, ymat, hmat)
    adv, deriv = along(held, from_left, from_right, adv)
    out = None
    x0 = 0
    for xs, halo in zip(CHUNKS, halos):
        out = outer(held, adv, halo, hmat, x0, out)
        x0 += xs
    return out, deriv


def solution(mesh):
    spec = P(None, "line", "cross", None)
    return jax.shard_map(
        on_device,
        mesh=mesh,
        in_specs=(spec,),
        out_specs=(spec, spec),
        check_vma=False,
    )
```

```python
import functools

import jax
import jax.numpy as jnp
import numpy as np
from jax import lax
from jax.experimental import pallas as pl
from jax.experimental.pallas import tpu as pltpu
from jax.sharding import PartitionSpec as P

ALPHA = 1.0 / 3.0
ROOT = (-1.0 + np.sqrt(1.0 - 4.0 * ALPHA * ALPHA)) / (2.0 * ALPHA)
KAPPA = -ALPHA / ROOT
NEAR = float(7.0 / 9.0 / KAPPA)
FAR = float(1.0 / 36.0 / KAPPA)
R = float(ROOT)
GAIN = float(1.0 / (1.0 - ROOT * ROOT))
TAPS = {1: 45.0, 2: -9.0, 3: 1.0, -1: -45.0, -2: 9.0, -3: -1.0}
UP = (16, 80, 32)
DOWN = (96, 32)
UP_STAGES = ((0, (0, 1)), (96, (2,)))
DOWN_STAGES = ((0, (0,)), (96, (1,)))
XB = 32
EB = 8
LANES = 128


def z_matrix(n):
    m = np.zeros((n, n), np.float32)
    for k, t in TAPS.items():
        for z in range(n):
            m[(z + k) % n, z] += t
    return m


def y_matrix(tile, xb):
    m = np.zeros((tile, tile), np.float32)
    for k, t in TAPS.items():
        for y in range(tile):
            if 0 <= y + k < tile:
                m[y, y + k] += t
    return np.kron(np.eye(xb, dtype=np.float32), m)


def halo_matrices(tile, xb):
    m = np.zeros((2, xb, tile, 3, xb), np.float32)
    for k, t in TAPS.items():
        for y in range(tile):
            for x in range(xb):
                if y + k < 0:
                    m[0, x, y, y + k + 3, x] += t
                if y + k >= tile:
                    m[1, x, y, y + k - tile, x] += t
    return m.reshape(2, xb * tile, 3 * xb)


def parity():
    return lax.rem(lax.axis_index("cross"), 2)


def split_dot(mat, val, flip=False):
    hi = val.astype(jnp.bfloat16)
    lo = (val - hi.astype(jnp.float32)).astype(jnp.bfloat16)
    if flip:
        return jnp.dot(hi, mat, preferred_element_type=jnp.float32) + jnp.dot(
            lo, mat, preferred_element_type=jnp.float32
        )
    return jnp.dot(mat, hi, preferred_element_type=jnp.float32) + jnp.dot(
        mat, lo, preferred_element_type=jnp.float32
    )


def pack_rows(held, out, first, row):
    comps, n, halves, tile, lanes = held.shape
    xs = out.shape[2]
    flat = held.reshape(comps * n * halves * tile, lanes)
    for c in range(comps):
        for half in range(halves):
            for y in range(3):
                start = ((c * n + row) * halves + half) * tile + first + y
                out[c, y, :, half * lanes : (half + 1) * lanes] = flat[
                    pl.ds(start, xs, stride=halves * tile)
                ]


def rows_of(held, c, rows):
    halves = held.shape[2]
    both = [held[c, rows, half].reshape(-1, LANES) for half in range(halves)]
    return jnp.concatenate(both, axis=1)


def put_rows(held, c, rows, val):
    halves, tile = held.shape[2:4]
    for half in range(halves):
        part = val[:, half * LANES : (half + 1) * LANES]
        held[c, rows, half] = part.reshape(-1, tile, LANES)


def halo_shape(vel, xs):
    comps, _, halves, _, lanes = vel.shape
    return pltpu.VMEM((comps, 3, xs, halves * lanes), jnp.float32)


def in_vmem(count):
    return [pl.BlockSpec(memory_space=pltpu.VMEM)] * count


def first_kernel(vel, up, buf, sem):
    xs = up.shape[2]
    cp = pltpu.make_async_copy(vel.at[:, pl.ds(0, xs)], buf, sem)
    cp.start()
    cp.wait()

    @pl.when(parity() == 1)
    def _():
        pack_rows(buf, up, buf.shape[3] - 3, 0)


def first(vel, xs):
    comps, _, halves, tile, lanes = vel.shape
    return pl.pallas_call(
        first_kernel,
        out_shape=halo_shape(vel, xs),
        in_specs=[pl.BlockSpec(memory_space=pltpu.HBM)],
        out_specs=pl.BlockSpec(memory_space=pltpu.VMEM),
        scratch_shapes=[
            pltpu.VMEM((comps, xs, halves, tile, lanes), jnp.float32),
            pltpu.SemaphoreType.DMA,
        ],
        compiler_params=pltpu.CompilerParams(vmem_limit_bytes=4 << 20),
        name="first",
    )(pltpu.with_memory_space_constraint(vel, pltpu.HBM))


def rest_kernel(vel, *outs):
    tile = vel.shape[3]
    side = parity()

    @pl.when(side == 1)
    def _():
        x0 = UP[0]
        for k, xs in enumerate(UP[1:]):
            pack_rows(vel, outs[k], tile - 3, x0)
            x0 += xs

    @pl.when(side == 0)
    def _():
        x0 = 0
        for k, xs in enumerate(DOWN):
            pack_rows(vel, outs[len(UP) - 1 + k], 0, x0)
            x0 += xs


def rest(vel):
    outs = [halo_shape(vel, xs) for xs in UP[1:] + DOWN]
    return pl.pallas_call(
        rest_kernel,
        out_shape=tuple(outs),
        in_specs=in_vmem(1),
        out_specs=in_vmem(len(outs)),
        compiler_params=pltpu.CompilerParams(vmem_limit_bytes=4 << 20),
        name="rest",
    )(vel)


def ends_kernel(vel, right, left, chip):
    n, tile = vel.shape[1], vel.shape[3]
    pack_rows(vel, chip, (1 - parity()) * (tile - 3), 0)

    def step(i, carry):
        _, p, _, t = carry
        return (p, vel[:, i] + R * p, t, vel[:, n - 1 - i] + R * t)

    def steps(b, carry):
        for j in range(8):
            carry = step(b * 8 + j, carry)
        return carry

    carry = (vel[:, 0], vel[:, 0], vel[:, n - 1], vel[:, n - 1])
    for i in range(1, 8):
        carry = step(i, carry)
    p_old, p, t_old, t = lax.fori_loop(1, n // 8, steps, carry)
    right[0] = p_old
    right[1] = p
    left[0] = GAIN * t
    left[1] = GAIN * (t_old + R * vel[:, 0])


def ends(vel):
    comps, nx, halves, tile, lanes = vel.shape
    out = pltpu.VMEM((2, comps, halves, tile, lanes), jnp.float32)
    return pl.pallas_call(
        ends_kernel,
        out_shape=(out, out, halo_shape(vel, nx)),
        in_specs=in_vmem(1),
        out_specs=in_vmem(3),
        compiler_params=pltpu.CompilerParams(vmem_limit_bytes=4 << 20),
        name="ends",
    )(vel)


def inner_kernel(vel, chip, zmat, ymat, hmat, adv):
    side = 1 - parity()
    comps, n, halves, _, lanes = vel.shape

    def block(b, _):
        rows = pl.ds(b * XB, XB)
        sv = rows_of(vel, 1, rows) * (-1.0 / 60.0)
        sw = rows_of(vel, 2, rows) * (-1.0 / 60.0)
        for c in range(comps):
            f = rows_of(vel, c, rows)
            gz = split_dot(zmat[...], f, flip=True)
            gy = split_dot(ymat[...], f)
            halo = chip[c, :, rows].reshape(-1, halves * lanes)
            gy = gy + split_dot(hmat[side], halo)
            put_rows(adv, c, rows, sv * gy + sw * gz)
        return 0

    lax.fori_loop(0, n // XB, block, 0)


def inner(vel, chip, zmat, ymat, hmat):
    return pl.pallas_call(
        inner_kernel,
        out_shape=pltpu.VMEM(vel.shape, jnp.float32),
        in_specs=in_vmem(5),
        out_specs=pl.BlockSpec(memory_space=pltpu.VMEM),
        compiler_params=pltpu.CompilerParams(vmem_limit_bytes=8 << 20),
        name="inner",
    )(vel, chip, zmat, ymat, hmat)


def along_kernel(vel, from_left, from_right, adv_in, adv, deriv_out, deriv, sems):
    n = vel.shape[1]

    def forward(b, p):
        for j in range(EB):
            i = b * EB + j
            p = vel[:, i] + R * p
            deriv[:, i] = p
        return p

    p_left = from_left[1]
    p_end = lax.fori_loop(0, n // EB, forward, p_left)
    h_n = from_right[0] + (GAIN * R) * p_end
    h_n1 = from_right[1] + (GAIN * R * R) * p_end
    h_a = deriv[:, n - 1] + R * h_n
    h_b = deriv[:, n - 2] + R * h_a

    def copy_out(b):
        rows = pl.ds(b * EB, EB)
        return pltpu.make_async_copy(deriv.at[:, rows], deriv_out.at[:, rows], sems.at[b])

    def backward(b, carry, last=False):
        h4, h3, h2, h1 = carry
        for j in range(EB):
            i = b * EB + EB - 1 - j
            if last and i < 2:
                p = p_left if i == 1 else from_left[0]
            else:
                p = deriv[:, i - 2]
            h = p + R * h1
            g = NEAR * (h3 - h1) + FAR * (h4 - h)
            deriv[:, i] = g
            adv[:, i] = adv_in[:, i] - vel[0, i][None] * g
            h4, h3, h2, h1 = h3, h2, h1, h
        copy_out(b).start()
        return (h4, h3, h2, h1)

    blocks = n // EB
    carry = lax.fori_loop(
        0, blocks - 1, lambda k, c: backward(blocks - 1 - k, c), (h_n1, h_n, h_a, h_b)
    )
    backward(0, carry, last=True)
    for b in range(blocks):
        copy_out(b).wait()


def along(vel, from_left, from_right, adv):
    return pl.pallas_call(
        along_kernel,
        out_shape=(
            pltpu.VMEM(vel.shape, jnp.float32),
            jax.ShapeDtypeStruct(vel.shape, jnp.float32),
        ),
        in_specs=in_vmem(4),
        out_specs=[
            pl.BlockSpec(memory_space=pltpu.VMEM),
            pl.BlockSpec(memory_space=pl.ANY),
        ],
        scratch_shapes=[
            pltpu.VMEM(vel.shape, jnp.float32),
            pltpu.SemaphoreType.DMA((vel.shape[1] // EB,)),
        ],
        input_output_aliases={3: 0},
        compiler_params=pltpu.CompilerParams(vmem_limit_bytes=8 << 20),
        name="along",
    )(vel, from_left, from_right, adv)


def outer_kernel(x0, side, sizes, *refs):
    vel, adv_in, hmat = refs[:3]
    pieces = refs[3 : 3 + len(sizes)]
    adv_out, adv, sems = refs[-3:]
    comps, xs, halves, _, lanes = adv.shape

    def take(c, at):
        parts = []
        need = XB
        for size, ref in zip(sizes, pieces):
            count = min(size - at, need)
            if count > 0:
                parts.append(ref[c, :, at : at + count])
                need -= count
                at = 0
            else:
                at -= size
        both = parts[0] if len(parts) == 1 else jnp.concatenate(parts, axis=1)
        return both.reshape(-1, halves * lanes)

    @pl.when(parity() == side)
    def _():
        copies = []
        for b in range(xs // XB):
            here = pl.ds(b * XB, XB)
            rows = pl.ds(x0 + b * XB, XB)
            sv = rows_of(vel, 1, rows) * (1.0 / 60.0)
            for c in range(comps):
                gy = split_dot(hmat[side], take(c, b * XB))
                put_rows(adv, c, here, rows_of(adv_in, c, rows) - sv * gy)
            copies.append(
                pltpu.make_async_copy(adv.at[:, here], adv_out.at[:, rows], sems.at[b])
            )
            copies[-1].start()
        for cp in copies:
            cp.wait()


def outer(vel, adv, hmat, pieces, x0, side, out):
    comps, _, halves, tile, lanes = vel.shape
    sizes = tuple(x.shape[2] for x in pieces)
    xs = sum(sizes)
    args = [vel, adv, hmat, *pieces]
    specs = in_vmem(len(args))
    alias = {}
    if out is not None:
        alias = {len(args): 0}
        args.append(out)
        specs.append(pl.BlockSpec(memory_space=pl.ANY))
    return pl.pallas_call(
        functools.partial(outer_kernel, x0, side, sizes),
        out_shape=jax.ShapeDtypeStruct(vel.shape, jnp.float32),
        in_specs=specs,
        out_specs=pl.BlockSpec(memory_space=pl.ANY),
        scratch_shapes=[
            pltpu.VMEM((comps, xs, halves, tile, lanes), jnp.float32),
            pltpu.SemaphoreType.DMA((xs // XB,)),
        ],
        input_output_aliases=alias,
        compiler_params=pltpu.CompilerParams(vmem_limit_bytes=8 << 20),
        name="outer",
    )(*args)


def send(x, axis, starts, step):
    count = lax.axis_size(axis)
    return lax.ppermute(x, axis, [(i, (i + s) % count) for i, s in zip(starts, step)])


def shift(x, axis, step):
    count = lax.axis_size(axis)
    return send(x, axis, range(count), [step] * count)


def swap(x, axis):
    count = lax.axis_size(axis)
    return send(x, axis, range(count), [1, -1] * (count // 2))


def on_device(velocity):
    comps, nx, tile, nz = velocity.shape
    halves = nz // LANES
    zmat = jnp.asarray(z_matrix(nz), jnp.bfloat16)
    ymat = jnp.asarray(y_matrix(tile, XB), jnp.bfloat16)
    hmat = jnp.asarray(halo_matrices(tile, XB), jnp.bfloat16)
    vel = velocity.reshape(comps, nx, tile, halves, LANES).transpose(0, 1, 3, 2, 4)
    up = [first(vel, UP[0])]
    sends = rest(vel)
    up += sends[: len(UP) - 1]
    down = sends[len(UP) - 1 :]
    lows = [shift(x, "cross", 1) for x in up]
    highs = [shift(x, "cross", -1) for x in down]
    right, left, chip = ends(vel)
    chip = swap(chip, "cross")
    from_left = shift(right, "line", 1)
    from_right = shift(left, "line", -1)
    adv = inner(vel, chip, zmat, ymat, hmat)
    adv, deriv = along(vel, from_left, from_right, adv)
    out = None
    for side, parts, stages in ((0, lows, UP_STAGES), (1, highs, DOWN_STAGES)):
        for x0, which in stages:
            out = outer(vel, adv, hmat, [parts[k] for k in which], x0, side, out)
    return tuple(
        v.transpose(0, 1, 3, 2, 4).reshape(velocity.shape) for v in (out, deriv)
    )


def solution(mesh):
    spec = P(None, "line", "cross", None)
    return jax.shard_map(
        on_device,
        mesh=mesh,
        in_specs=(spec,),
        out_specs=(spec, spec),
        check_vma=False,
    )
```

```python
import functools

import jax
import jax.numpy as jnp
import numpy as np
from jax import lax
from jax.experimental import pallas as pl
from jax.experimental.pallas import tpu as pltpu
from jax.sharding import PartitionSpec as P

ALPHA = 1.0 / 3.0
ROOT = (-1.0 + np.sqrt(1.0 - 4.0 * ALPHA * ALPHA)) / (2.0 * ALPHA)
KAPPA = -ALPHA / ROOT
NEAR = float(7.0 / 9.0 / KAPPA)
FAR = float(1.0 / 36.0 / KAPPA)
R = float(ROOT)
GAIN = float(1.0 / (1.0 - ROOT * ROOT))
TAPS = {1: 45.0, 2: -9.0, 3: 1.0, -1: -45.0, -2: 9.0, -3: -1.0}
UP = (16, 88, 24)
DOWN = (104, 24)
UP_STAGES = ((0, (0, 1)), (104, (2,)))
DOWN_STAGES = ((0, (0,)), (104, (1,)))
XB = 16
OB = 8
EB = 8
LANES = 128


def z_matrix(n):
    m = np.zeros((n, n), np.float32)
    for k, t in TAPS.items():
        for z in range(n):
            m[(z + k) % n, z] += t
    return m


def y_matrix(tile, xb):
    m = np.zeros((tile, tile), np.float32)
    for k, t in TAPS.items():
        for y in range(tile):
            if 0 <= y + k < tile:
                m[y, y + k] += t
    return np.kron(np.eye(xb, dtype=np.float32), m)


def halo_matrices(tile, xb):
    m = np.zeros((2, xb, tile, 3, xb), np.float32)
    for k, t in TAPS.items():
        for y in range(tile):
            for x in range(xb):
                if y + k < 0:
                    m[0, x, y, y + k + 3, x] += t
                if y + k >= tile:
                    m[1, x, y, y + k - tile, x] += t
    return m.reshape(2, xb * tile, 3 * xb)


def parity():
    return lax.rem(lax.axis_index("cross"), 2)


def split_dot(mat, val, flip=False):
    hi = val.astype(jnp.bfloat16)
    lo = (val - hi.astype(jnp.float32)).astype(jnp.bfloat16)
    if flip:
        return jnp.dot(hi, mat, preferred_element_type=jnp.float32) + jnp.dot(
            lo, mat, preferred_element_type=jnp.float32
        )
    return jnp.dot(mat, hi, preferred_element_type=jnp.float32) + jnp.dot(
        mat, lo, preferred_element_type=jnp.float32
    )


def pack_rows(held, out, first, row):
    comps, n, halves, tile, lanes = held.shape
    xs = out.shape[2]
    flat = held.reshape(comps * n * halves * tile, lanes)
    for c in range(comps):
        for half in range(halves):
            for y in range(3):
                start = ((c * n + row) * halves + half) * tile + first + y
                out[c, y, :, half * lanes : (half + 1) * lanes] = flat[
                    pl.ds(start, xs, stride=halves * tile)
                ]


def rows_of(held, c, rows):
    halves = held.shape[2]
    both = [held[c, rows, half].reshape(-1, LANES) for half in range(halves)]
    return jnp.concatenate(both, axis=1)


def put_rows(held, c, rows, val):
    halves, tile = held.shape[2:4]
    for half in range(halves):
        part = val[:, half * LANES : (half + 1) * LANES]
        held[c, rows, half] = part.reshape(-1, tile, LANES)


def halo_shape(vel, xs):
    comps, _, halves, _, lanes = vel.shape
    return pltpu.VMEM((comps, 3, xs, halves * lanes), jnp.float32)


def in_vmem(count):
    return [pl.BlockSpec(memory_space=pltpu.VMEM)] * count


def first_kernel(vel, up, buf, sem):
    xs = up.shape[2]
    cp = pltpu.make_async_copy(vel.at[:, pl.ds(0, xs)], buf, sem)
    cp.start()
    cp.wait()

    @pl.when(parity() == 1)
    def _():
        pack_rows(buf, up, buf.shape[3] - 3, 0)


def first(vel, xs):
    comps, _, halves, tile, lanes = vel.shape
    return pl.pallas_call(
        first_kernel,
        out_shape=halo_shape(vel, xs),
        in_specs=[pl.BlockSpec(memory_space=pltpu.HBM)],
        out_specs=pl.BlockSpec(memory_space=pltpu.VMEM),
        scratch_shapes=[
            pltpu.VMEM((comps, xs, halves, tile, lanes), jnp.float32),
            pltpu.SemaphoreType.DMA,
        ],
        compiler_params=pltpu.CompilerParams(vmem_limit_bytes=4 << 20),
        name="first",
    )(pltpu.with_memory_space_constraint(vel, pltpu.HBM))


def rest_kernel(vel, *outs):
    tile = vel.shape[3]
    side = parity()

    @pl.when(side == 1)
    def _():
        x0 = UP[0]
        for k, xs in enumerate(UP[1:]):
            pack_rows(vel, outs[k], tile - 3, x0)
            x0 += xs

    @pl.when(side == 0)
    def _():
        x0 = 0
        for k, xs in enumerate(DOWN):
            pack_rows(vel, outs[len(UP) - 1 + k], 0, x0)
            x0 += xs


def rest(vel):
    outs = [halo_shape(vel, xs) for xs in UP[1:] + DOWN]
    return pl.pallas_call(
        rest_kernel,
        out_shape=tuple(outs),
        in_specs=in_vmem(1),
        out_specs=in_vmem(len(outs)),
        compiler_params=pltpu.CompilerParams(vmem_limit_bytes=4 << 20),
        name="rest",
    )(vel)


def ends_kernel(vel, right, left, chip):
    n, tile = vel.shape[1], vel.shape[3]
    pack_rows(vel, chip, (1 - parity()) * (tile - 3), 0)

    def step(i, carry):
        _, p, _, t = carry
        return (p, vel[:, i] + R * p, t, vel[:, n - 1 - i] + R * t)

    def steps(b, carry):
        for j in range(8):
            carry = step(b * 8 + j, carry)
        return carry

    carry = (vel[:, 0], vel[:, 0], vel[:, n - 1], vel[:, n - 1])
    for i in range(1, 8):
        carry = step(i, carry)
    p_old, p, t_old, t = lax.fori_loop(1, n // 8, steps, carry)
    right[0] = p_old
    right[1] = p
    left[0] = GAIN * t
    left[1] = GAIN * (t_old + R * vel[:, 0])


def ends(vel):
    comps, nx, halves, tile, lanes = vel.shape
    out = pltpu.VMEM((2, comps, halves, tile, lanes), jnp.float32)
    return pl.pallas_call(
        ends_kernel,
        out_shape=(out, out, halo_shape(vel, nx)),
        in_specs=in_vmem(1),
        out_specs=in_vmem(3),
        compiler_params=pltpu.CompilerParams(vmem_limit_bytes=4 << 20),
        name="ends",
    )(vel)


def inner_kernel(vel, chip, zmat, ymat, adv):
    comps, n, halves, _, lanes = vel.shape
    side = 1 - parity()

    def block(b, _):
        rows = pl.ds(b * XB, XB)
        sv = rows_of(vel, 1, rows) * (-1.0 / 60.0)
        sw = rows_of(vel, 2, rows) * (-1.0 / 60.0)
        for c in range(comps):
            f = rows_of(vel, c, rows)
            gz = split_dot(zmat[...], f, flip=True)
            halo = chip[c, :, rows].reshape(-1, halves * lanes)
            gy = split_dot(ymat[side], jnp.concatenate([f, halo], axis=0))
            put_rows(adv, c, rows, sv * gy + sw * gz)
        return 0

    lax.fori_loop(0, n // XB, block, 0)


def inner(vel, chip, zmat, ymat):
    return pl.pallas_call(
        inner_kernel,
        out_shape=pltpu.VMEM(vel.shape, jnp.float32),
        in_specs=in_vmem(4),
        out_specs=pl.BlockSpec(memory_space=pltpu.VMEM),
        compiler_params=pltpu.CompilerParams(vmem_limit_bytes=8 << 20),
        name="inner",
    )(vel, chip, zmat, ymat)


def along_kernel(vel, from_left, from_right, adv_in, adv, deriv_out, deriv, sems):
    n = vel.shape[1]

    def forward(b, p):
        for j in range(EB):
            i = b * EB + j
            p = vel[:, i] + R * p
            deriv[:, i] = p
        return p

    p_left = from_left[1]
    p_end = lax.fori_loop(0, n // EB, forward, p_left)
    h_n = from_right[0] + (GAIN * R) * p_end
    h_n1 = from_right[1] + (GAIN * R * R) * p_end
    h_a = deriv[:, n - 1] + R * h_n
    h_b = deriv[:, n - 2] + R * h_a

    def copy_out(b):
        rows = pl.ds(b * EB, EB)
        return pltpu.make_async_copy(deriv.at[:, rows], deriv_out.at[:, rows], sems.at[b])

    def backward(b, carry, last=False):
        h4, h3, h2, h1 = carry
        for j in range(EB):
            i = b * EB + EB - 1 - j
            if last and i < 2:
                p = p_left if i == 1 else from_left[0]
            else:
                p = deriv[:, i - 2]
            h = p + R * h1
            g = NEAR * (h3 - h1) + FAR * (h4 - h)
            deriv[:, i] = g
            adv[:, i] = adv_in[:, i] - vel[0, i][None] * g
            h4, h3, h2, h1 = h3, h2, h1, h
        copy_out(b).start()
        return (h4, h3, h2, h1)

    blocks = n // EB
    carry = lax.fori_loop(
        0, blocks - 1, lambda k, c: backward(blocks - 1 - k, c), (h_n1, h_n, h_a, h_b)
    )
    backward(0, carry, last=True)
    for b in range(blocks):
        copy_out(b).wait()


def along(vel, from_left, from_right, adv):
    return pl.pallas_call(
        along_kernel,
        out_shape=(
            pltpu.VMEM(vel.shape, jnp.float32),
            jax.ShapeDtypeStruct(vel.shape, jnp.float32),
        ),
        in_specs=in_vmem(4),
        out_specs=[
            pl.BlockSpec(memory_space=pltpu.VMEM),
            pl.BlockSpec(memory_space=pl.ANY),
        ],
        scratch_shapes=[
            pltpu.VMEM(vel.shape, jnp.float32),
            pltpu.SemaphoreType.DMA((vel.shape[1] // EB,)),
        ],
        input_output_aliases={3: 0},
        compiler_params=pltpu.CompilerParams(vmem_limit_bytes=8 << 20),
        name="along",
    )(vel, from_left, from_right, adv)


def outer_kernel(x0, side, sizes, *refs):
    vel, adv_in, hmat = refs[:3]
    pieces = refs[3 : 3 + len(sizes)]
    adv_out, adv, sems = refs[-3:]
    comps, xs, halves, _, lanes = adv.shape

    span = OB if xs <= 32 else 4 * OB

    def take(c, at):
        for size, ref in zip(sizes, pieces):
            if at < size:
                return ref[c, :, at : at + OB].reshape(-1, halves * lanes)
            at -= size

    @pl.when(parity() == side)
    def _():
        copies = []
        for start in range(0, xs, span):
            count = min(span, xs - start)
            for at in range(start, start + count, OB):
                rows = pl.ds(x0 + at, OB)
                sv = rows_of(vel, 1, rows) * (1.0 / 60.0)
                for c in range(comps):
                    gy = split_dot(hmat[side], take(c, at))
                    put_rows(
                        adv, c, pl.ds(at, OB), rows_of(adv_in, c, rows) - sv * gy
                    )
            copies.append(
                pltpu.make_async_copy(
                    adv.at[:, pl.ds(start, count)],
                    adv_out.at[:, pl.ds(x0 + start, count)],
                    sems.at[start // span],
                )
            )
            copies[-1].start()
        for cp in copies:
            cp.wait()


def outer(vel, adv, hmat, pieces, x0, side, out):
    comps, _, halves, tile, lanes = vel.shape
    sizes = tuple(x.shape[2] for x in pieces)
    xs = sum(sizes)
    args = [vel, adv, hmat, *pieces]
    specs = in_vmem(len(args))
    alias = {}
    if out is not None:
        alias = {len(args): 0}
        args.append(out)
        specs.append(pl.BlockSpec(memory_space=pl.ANY))
    return pl.pallas_call(
        functools.partial(outer_kernel, x0, side, sizes),
        out_shape=jax.ShapeDtypeStruct(vel.shape, jnp.float32),
        in_specs=specs,
        out_specs=pl.BlockSpec(memory_space=pl.ANY),
        scratch_shapes=[
            pltpu.VMEM((comps, xs, halves, tile, lanes), jnp.float32),
            pltpu.SemaphoreType.DMA((4,)),
        ],
        input_output_aliases=alias,
        compiler_params=pltpu.CompilerParams(vmem_limit_bytes=8 << 20),
        name="outer",
    )(*args)


def send(x, axis, starts, step):
    count = lax.axis_size(axis)
    return lax.ppermute(x, axis, [(i, (i + s) % count) for i, s in zip(starts, step)])


def shift(x, axis, step):
    count = lax.axis_size(axis)
    return send(x, axis, range(count), [step] * count)


def swap(x, axis):
    count = lax.axis_size(axis)
    return send(x, axis, range(count), [1, -1] * (count // 2))


def on_device(velocity):
    comps, nx, tile, nz = velocity.shape
    halves = nz // LANES
    zmat = jnp.asarray(z_matrix(nz), jnp.bfloat16)
    both = [np.concatenate([y_matrix(tile, XB), m], 1) for m in halo_matrices(tile, XB)]
    ymat = jnp.asarray(np.stack(both), jnp.bfloat16)
    omat = jnp.asarray(halo_matrices(tile, OB), jnp.bfloat16)
    vel = velocity.reshape(comps, nx, tile, halves, LANES).transpose(0, 1, 3, 2, 4)
    up = [first(vel, UP[0])]
    sends = rest(vel)
    up += sends[: len(UP) - 1]
    down = sends[len(UP) - 1 :]
    lows = [shift(x, "cross", 1) for x in up]
    highs = [shift(x, "cross", -1) for x in down]
    right, left, chip = ends(vel)
    chip = swap(chip, "cross")
    from_left = shift(right, "line", 1)
    from_right = shift(left, "line", -1)
    adv = inner(vel, chip, zmat, ymat)
    adv, deriv = along(vel, from_left, from_right, adv)
    out = None
    for side, parts, stages in ((0, lows, UP_STAGES), (1, highs, DOWN_STAGES)):
        for x0, which in stages:
            out = outer(vel, adv, omat, [parts[k] for k in which], x0, side, out)
    return tuple(
        v.transpose(0, 1, 3, 2, 4).reshape(velocity.shape) for v in (out, deriv)
    )


def solution(mesh):
    spec = P(None, "line", "cross", None)
    return jax.shard_map(
        on_device,
        mesh=mesh,
        in_specs=(spec,),
        out_specs=(spec, spec),
        check_vma=False,
    )
```

```python
import functools

import jax
import jax.numpy as jnp
import numpy as np
from jax import lax
from jax.experimental import pallas as pl
from jax.experimental.pallas import tpu as pltpu
from jax.sharding import PartitionSpec as P

ALPHA = 1.0 / 3.0
ROOT = (-1.0 + np.sqrt(1.0 - 4.0 * ALPHA * ALPHA)) / (2.0 * ALPHA)
KAPPA = -ALPHA / ROOT
NEAR = float(7.0 / 9.0 / KAPPA)
FAR = float(1.0 / 36.0 / KAPPA)
R = float(ROOT)
GAIN = float(1.0 / (1.0 - ROOT * ROOT))
TAPS = {1: 45.0, 2: -9.0, 3: 1.0, -1: -45.0, -2: 9.0, -3: -1.0}
UP = (16, 88, 24)
DOWN = (104, 24)
UP_STAGES = ((0, (0, 1)), (104, (2,)))
DOWN_STAGES = ((0, (0,)), (104, (1,)))
XB = 16
UNROLL = 8
OB = 8
EB = 8
LANES = 128


def z_matrix(n):
    m = np.zeros((n, n), np.float32)
    for k, t in TAPS.items():
        for z in range(n):
            m[(z + k) % n, z] += t
    return m


def y_matrix(tile, xb):
    m = np.zeros((tile, tile), np.float32)
    for k, t in TAPS.items():
        for y in range(tile):
            if 0 <= y + k < tile:
                m[y, y + k] += t
    return np.kron(np.eye(xb, dtype=np.float32), m)


def halo_matrices(tile, xb):
    m = np.zeros((2, xb, tile, 3, xb), np.float32)
    for k, t in TAPS.items():
        for y in range(tile):
            for x in range(xb):
                if y + k < 0:
                    m[0, x, y, y + k + 3, x] += t
                if y + k >= tile:
                    m[1, x, y, y + k - tile, x] += t
    return m.reshape(2, xb * tile, 3 * xb)


def parity():
    return lax.rem(lax.axis_index("cross"), 2)


def split(val):
    hi = val.astype(jnp.bfloat16)
    return hi, (val - hi.astype(jnp.float32)).astype(jnp.bfloat16)


def dot(a, b):
    return jnp.dot(a, b, preferred_element_type=jnp.float32)


def split_dot(mat, val):
    hi, lo = split(val)
    return dot(mat, hi) + dot(mat, lo)


def halo_weights(tile):
    m = halo_matrices(tile, 1).reshape(2, tile, 3).transpose(0, 2, 1) / 60.0
    return np.repeat(m[..., None], LANES, axis=3)


def pack_rows(held, out, first, row):
    comps, n, halves, tile, lanes = held.shape
    xs = out.shape[3]
    flat = held.reshape(comps * n * halves * tile, lanes)
    for c in range(comps):
        for half in range(halves):
            for y in range(3):
                start = ((c * n + row) * halves + half) * tile + first + y
                out[c, y, half] = flat[
                    pl.ds(start, xs, stride=halves * tile)
                ]


def rows_of(held, c, rows):
    halves = held.shape[2]
    both = [held[c, rows, half].reshape(-1, LANES) for half in range(halves)]
    return jnp.concatenate(both, axis=1)


def halo_of(halo, c, rows):
    both = [halo[c, :, half, rows].reshape(-1, LANES) for half in range(halo.shape[2])]
    return jnp.concatenate(both, axis=1)


def put_rows(held, c, rows, val):
    halves, tile = held.shape[2:4]
    for half in range(halves):
        part = val[:, half * LANES : (half + 1) * LANES]
        held[c, rows, half] = part.reshape(-1, tile, LANES)


def halo_shape(vel, xs):
    comps, _, halves, _, lanes = vel.shape
    return pltpu.VMEM((comps, 3, halves, xs, lanes), jnp.float32)


def in_vmem(count):
    return [pl.BlockSpec(memory_space=pltpu.VMEM)] * count


def first_kernel(vel, up, buf, sem):
    xs = up.shape[3]

    @pl.when(parity() == 1)
    def _():
        cp = pltpu.make_async_copy(vel.at[:, pl.ds(0, xs)], buf, sem)
        cp.start()
        cp.wait()
        pack_rows(buf, up, buf.shape[3] - 3, 0)


def first(vel, xs):
    comps, _, halves, tile, lanes = vel.shape
    return pl.pallas_call(
        first_kernel,
        out_shape=halo_shape(vel, xs),
        in_specs=[pl.BlockSpec(memory_space=pltpu.HBM)],
        out_specs=pl.BlockSpec(memory_space=pltpu.VMEM),
        scratch_shapes=[
            pltpu.VMEM((comps, xs, halves, tile, lanes), jnp.float32),
            pltpu.SemaphoreType.DMA,
        ],
        compiler_params=pltpu.CompilerParams(vmem_limit_bytes=4 << 20),
        name="first",
    )(pltpu.with_memory_space_constraint(vel, pltpu.HBM))


def rest_kernel(vel, *outs):
    tile = vel.shape[3]
    side = parity()

    @pl.when(side == 1)
    def _():
        x0 = UP[0]
        for k, xs in enumerate(UP[1:]):
            pack_rows(vel, outs[k], tile - 3, x0)
            x0 += xs

    @pl.when(side == 0)
    def _():
        x0 = 0
        for k, xs in enumerate(DOWN):
            pack_rows(vel, outs[len(UP) - 1 + k], 0, x0)
            x0 += xs


def rest(vel):
    outs = [halo_shape(vel, xs) for xs in UP[1:] + DOWN]
    return pl.pallas_call(
        rest_kernel,
        out_shape=tuple(outs),
        in_specs=in_vmem(1),
        out_specs=in_vmem(len(outs)),
        compiler_params=pltpu.CompilerParams(vmem_limit_bytes=4 << 20),
        name="rest",
    )(vel)


def ends_kernel(vel, right, left, chip):
    n, tile = vel.shape[1], vel.shape[3]
    pack_rows(vel, chip, (1 - parity()) * (tile - 3), 0)

    def step(i, carry):
        _, p, _, t = carry
        return (p, vel[:, i] + R * p, t, vel[:, n - 1 - i] + R * t)

    def steps(b, carry):
        for j in range(8):
            carry = step(b * 8 + j, carry)
        return carry

    carry = (vel[:, 0], vel[:, 0], vel[:, n - 1], vel[:, n - 1])
    for i in range(1, 8):
        carry = step(i, carry)
    p_old, p, t_old, t = lax.fori_loop(1, n // 8, steps, carry)
    right[0] = p_old
    right[1] = p
    left[0] = GAIN * t
    left[1] = GAIN * (t_old + R * vel[:, 0])


def ends(vel):
    comps, nx, halves, tile, lanes = vel.shape
    out = pltpu.VMEM((2, comps, halves, tile, lanes), jnp.float32)
    return pl.pallas_call(
        ends_kernel,
        out_shape=(out, out, halo_shape(vel, nx)),
        in_specs=in_vmem(1),
        out_specs=in_vmem(3),
        compiler_params=pltpu.CompilerParams(vmem_limit_bytes=4 << 20),
        name="ends",
    )(vel)


def inner_kernel(vel, chip, zmat, ymat, adv):
    comps, n, _, tile, _ = vel.shape
    side = 1 - parity()

    def block(b, _):
        rows = pl.ds(b * XB, XB)
        sv = rows_of(vel, 1, rows) * (-1.0 / 60.0)
        sw = rows_of(vel, 2, rows) * (-1.0 / 60.0)
        size = XB * tile
        parts = [split(rows_of(vel, c, rows)) for c in range(comps)]
        stack = [p[0] for p in parts] + [p[1] for p in parts]
        gz = dot(jnp.concatenate(stack, axis=0), zmat[...])
        for c in range(comps):
            halo = split(halo_of(chip, c, rows))
            gy = [
                dot(ymat[side], jnp.concatenate([p, h], axis=0))
                for p, h in zip(parts[c], halo)
            ]
            low = gz[(comps + c) * size : (comps + c + 1) * size]
            along_z = gz[c * size : (c + 1) * size] + low
            put_rows(adv, c, rows, sv * (gy[0] + gy[1]) + sw * along_z)
        return 0

    lax.fori_loop(0, n // XB, block, 0, unroll=UNROLL)


def inner(vel, chip, zmat, ymat):
    return pl.pallas_call(
        inner_kernel,
        out_shape=pltpu.VMEM(vel.shape, jnp.float32),
        in_specs=in_vmem(4),
        out_specs=pl.BlockSpec(memory_space=pltpu.VMEM),
        compiler_params=pltpu.CompilerParams(vmem_limit_bytes=8 << 20),
        name="inner",
    )(vel, chip, zmat, ymat)


def along_kernel(vel, from_left, from_right, adv_in, adv, deriv_out, deriv, sems):
    n = vel.shape[1]

    def forward(b, p):
        for j in range(EB):
            i = b * EB + j
            p = vel[:, i] + R * p
            deriv[:, i] = p
        return p

    p_left = from_left[1]
    p_end = lax.fori_loop(0, n // EB, forward, p_left)
    h_n = from_right[0] + (GAIN * R) * p_end
    h_n1 = from_right[1] + (GAIN * R * R) * p_end
    h_a = deriv[:, n - 1] + R * h_n
    h_b = deriv[:, n - 2] + R * h_a

    def copy_out(b):
        rows = pl.ds(b * EB, EB)
        return pltpu.make_async_copy(deriv.at[:, rows], deriv_out.at[:, rows], sems.at[b])

    def backward(b, carry, last=False):
        h4, h3, h2, h1 = carry
        for j in range(EB):
            i = b * EB + EB - 1 - j
            if last and i < 2:
                p = p_left if i == 1 else from_left[0]
            else:
                p = deriv[:, i - 2]
            h = p + R * h1
            g = NEAR * (h3 - h1) + FAR * (h4 - h)
            deriv[:, i] = g
            adv[:, i] = adv_in[:, i] - vel[0, i][None] * g
            h4, h3, h2, h1 = h3, h2, h1, h
        copy_out(b).start()
        return (h4, h3, h2, h1)

    blocks = n // EB
    carry = lax.fori_loop(
        0, blocks - 1, lambda k, c: backward(blocks - 1 - k, c), (h_n1, h_n, h_a, h_b)
    )
    backward(0, carry, last=True)
    for b in range(blocks):
        copy_out(b).wait()


def along(vel, from_left, from_right, adv):
    return pl.pallas_call(
        along_kernel,
        out_shape=(
            pltpu.VMEM(vel.shape, jnp.float32),
            jax.ShapeDtypeStruct(vel.shape, jnp.float32),
        ),
        in_specs=in_vmem(4),
        out_specs=[
            pl.BlockSpec(memory_space=pltpu.VMEM),
            pl.BlockSpec(memory_space=pl.ANY),
        ],
        scratch_shapes=[
            pltpu.VMEM(vel.shape, jnp.float32),
            pltpu.SemaphoreType.DMA((vel.shape[1] // EB,)),
        ],
        input_output_aliases={3: 0},
        compiler_params=pltpu.CompilerParams(vmem_limit_bytes=8 << 20),
        name="along",
    )(vel, from_left, from_right, adv)


def outer_kernel(x0, side, sizes, *refs):
    vel, adv_in, hmat, weights = refs[:4]
    pieces = refs[4 : 4 + len(sizes)]
    adv_out, adv, sems = refs[-3:]
    comps, xs, halves, tile, lanes = adv.shape

    short = len(sizes) == 1 and xs <= 32
    span = OB if short else 4 * OB

    def take(c, at):
        for size, ref in zip(sizes, pieces):
            if at < size:
                return halo_of(ref, c, slice(at, at + OB))
            at -= size

    def by_row(x):
        flat = pieces[0].reshape(comps * 3 * halves * xs, lanes)
        for half in range(halves):
            v = vel[1, x0 + x, half]
            for c in range(comps):
                gy = None
                for y in range(3):
                    at = ((c * 3 + y) * halves + half) * xs + x
                    term = weights[side, y] * flat[pl.ds(at, tile, stride=0)]
                    gy = term if gy is None else gy + term
                adv[c, x, half] = adv_in[c, x0 + x, half] - v * gy

    @pl.when(parity() == side)
    def _():
        copies = []
        for start in range(0, xs, span):
            count = min(span, xs - start)
            for at in range(start, start + count, OB):
                rows = pl.ds(x0 + at, OB)
                if short:
                    for x in range(at, at + OB):
                        by_row(x)
                    continue
                sv = rows_of(vel, 1, rows) * (1.0 / 60.0)
                for c in range(comps):
                    gy = split_dot(hmat[side], take(c, at))
                    put_rows(
                        adv, c, pl.ds(at, OB), rows_of(adv_in, c, rows) - sv * gy
                    )
            copies.append(
                pltpu.make_async_copy(
                    adv.at[:, pl.ds(start, count)],
                    adv_out.at[:, pl.ds(x0 + start, count)],
                    sems.at[start // span],
                )
            )
            copies[-1].start()
        for cp in copies:
            cp.wait()


def outer(vel, adv, hmat, weights, pieces, x0, side, out):
    comps, _, halves, tile, lanes = vel.shape
    sizes = tuple(x.shape[3] for x in pieces)
    xs = sum(sizes)
    args = [vel, adv, hmat, weights, *pieces]
    specs = in_vmem(len(args))
    alias = {}
    if out is not None:
        alias = {len(args): 0}
        args.append(out)
        specs.append(pl.BlockSpec(memory_space=pl.ANY))
    return pl.pallas_call(
        functools.partial(outer_kernel, x0, side, sizes),
        out_shape=jax.ShapeDtypeStruct(vel.shape, jnp.float32),
        in_specs=specs,
        out_specs=pl.BlockSpec(memory_space=pl.ANY),
        scratch_shapes=[
            pltpu.VMEM((comps, xs, halves, tile, lanes), jnp.float32),
            pltpu.SemaphoreType.DMA((8,)),
        ],
        input_output_aliases=alias,
        compiler_params=pltpu.CompilerParams(vmem_limit_bytes=8 << 20),
        name="outer",
    )(*args)


def send(x, axis, starts, step):
    count = lax.axis_size(axis)
    return lax.ppermute(x, axis, [(i, (i + s) % count) for i, s in zip(starts, step)])


def shift(x, axis, step):
    count = lax.axis_size(axis)
    return send(x, axis, range(count), [step] * count)


def swap(x, axis):
    count = lax.axis_size(axis)
    return send(x, axis, range(count), [1, -1] * (count // 2))


def on_device(velocity):
    comps, nx, tile, nz = velocity.shape
    halves = nz // LANES
    zmat = jnp.asarray(z_matrix(nz), jnp.bfloat16)
    both = [np.concatenate([y_matrix(tile, XB), m], 1) for m in halo_matrices(tile, XB)]
    ymat = jnp.asarray(np.stack(both), jnp.bfloat16)
    weights = jnp.asarray(halo_weights(tile), jnp.float32)
    omat = jnp.asarray(halo_matrices(tile, OB), jnp.bfloat16)
    vel = velocity.reshape(comps, nx, tile, halves, LANES).transpose(0, 1, 3, 2, 4)
    up = [first(vel, UP[0])]
    sends = rest(vel)
    up += sends[: len(UP) - 1]
    down = sends[len(UP) - 1 :]
    lows = [shift(x, "cross", 1) for x in up]
    highs = [shift(x, "cross", -1) for x in down]
    right, left, chip = ends(vel)
    chip = swap(chip, "cross")
    from_left = shift(right, "line", 1)
    from_right = shift(left, "line", -1)
    adv = inner(vel, chip, zmat, ymat)
    adv, deriv = along(vel, from_left, from_right, adv)
    out = None
    for side, parts, stages in ((0, lows, UP_STAGES), (1, highs, DOWN_STAGES)):
        for x0, which in stages:
            out = outer(vel, adv, omat, weights, [parts[k] for k in which], x0, side, out)
    return tuple(
        v.transpose(0, 1, 3, 2, 4).reshape(velocity.shape) for v in (out, deriv)
    )


def solution(mesh):
    spec = P(None, "line", "cross", None)
    return jax.shard_map(
        on_device,
        mesh=mesh,
        in_specs=(spec,),
        out_specs=(spec, spec),
        check_vma=False,
    )
```

```python
import functools

import jax
import jax.numpy as jnp
import numpy as np
from jax import lax
from jax.experimental import pallas as pl
from jax.experimental.pallas import tpu as pltpu
from jax.sharding import PartitionSpec as P

ALPHA = 1.0 / 3.0
ROOT = (-1.0 + np.sqrt(1.0 - 4.0 * ALPHA * ALPHA)) / (2.0 * ALPHA)
KAPPA = -ALPHA / ROOT
NEAR = float(7.0 / 9.0 / KAPPA)
FAR = float(1.0 / 36.0 / KAPPA)
R = float(ROOT)
GAIN = float(1.0 / (1.0 - ROOT * ROOT))
TAPS = {1: 45.0, 2: -9.0, 3: 1.0, -1: -45.0, -2: 9.0, -3: -1.0}
UP = (16, 88, 24)
DOWN = (104, 24)
UP_STAGES = ((0, (0, 1)), (104, (2,)))
DOWN_STAGES = ((0, (0,)), (104, (1,)))
XB = 16
UNROLL = 8
OB = 8
EB = 8
LANES = 128


def z_matrix(n):
    m = np.zeros((n, n), np.float32)
    for k, t in TAPS.items():
        for z in range(n):
            m[(z + k) % n, z] += t
    return m


def y_matrix(tile, xb):
    m = np.zeros((tile, tile), np.float32)
    for k, t in TAPS.items():
        for y in range(tile):
            if 0 <= y + k < tile:
                m[y, y + k] += t
    return np.kron(np.eye(xb, dtype=np.float32), m)


def halo_matrices(tile, xb):
    m = np.zeros((2, xb, tile, 3, xb), np.float32)
    for k, t in TAPS.items():
        for y in range(tile):
            for x in range(xb):
                if y + k < 0:
                    m[0, x, y, y + k + 3, x] += t
                if y + k >= tile:
                    m[1, x, y, y + k - tile, x] += t
    return m.reshape(2, xb * tile, 3 * xb)


def parity():
    return lax.rem(lax.axis_index("cross"), 2)


def split(val):
    hi = val.astype(jnp.bfloat16)
    return hi, (val - hi.astype(jnp.float32)).astype(jnp.bfloat16)


def dot(a, b):
    return jnp.dot(a, b, preferred_element_type=jnp.float32)


def split_dot(mat, val):
    hi, lo = split(val)
    return dot(mat, hi) + dot(mat, lo)


def pack_rows(held, out, first, row):
    comps, n, halves, tile, lanes = held.shape
    xs = out.shape[2]
    flat = held.reshape(comps * n * halves * tile, lanes)
    for c in range(comps):
        for half in range(halves):
            for y in range(3):
                start = ((c * n + row) * halves + half) * tile + first + y
                out[c, y, :, half * lanes : (half + 1) * lanes] = flat[
                    pl.ds(start, xs, stride=halves * tile)
                ]


def rows_of(held, c, rows):
    halves = held.shape[2]
    both = [held[c, rows, half].reshape(-1, LANES) for half in range(halves)]
    return jnp.concatenate(both, axis=1)


def put_rows(held, c, rows, val):
    halves, tile = held.shape[2:4]
    for half in range(halves):
        part = val[:, half * LANES : (half + 1) * LANES]
        held[c, rows, half] = part.reshape(-1, tile, LANES)


def halo_shape(vel, xs):
    comps, _, halves, _, lanes = vel.shape
    return pltpu.VMEM((comps, 3, xs, halves * lanes), jnp.float32)


def in_vmem(count):
    return [pl.BlockSpec(memory_space=pltpu.VMEM)] * count


def first_kernel(vel, up, buf, sem):
    xs = up.shape[2]

    @pl.when(parity() == 1)
    def _():
        cp = pltpu.make_async_copy(vel.at[:, pl.ds(0, xs)], buf, sem)
        cp.start()
        cp.wait()
        pack_rows(buf, up, buf.shape[3] - 3, 0)


def first(vel, xs):
    comps, _, halves, tile, lanes = vel.shape
    return pl.pallas_call(
        first_kernel,
        out_shape=halo_shape(vel, xs),
        in_specs=[pl.BlockSpec(memory_space=pltpu.HBM)],
        out_specs=pl.BlockSpec(memory_space=pltpu.VMEM),
        scratch_shapes=[
            pltpu.VMEM((comps, xs, halves, tile, lanes), jnp.float32),
            pltpu.SemaphoreType.DMA,
        ],
        compiler_params=pltpu.CompilerParams(vmem_limit_bytes=4 << 20),
        name="first",
    )(pltpu.with_memory_space_constraint(vel, pltpu.HBM))


def rest_kernel(vel, *outs):
    tile = vel.shape[3]
    side = parity()

    @pl.when(side == 1)
    def _():
        x0 = UP[0]
        for k, xs in enumerate(UP[1:]):
            pack_rows(vel, outs[k], tile - 3, x0)
            x0 += xs

    @pl.when(side == 0)
    def _():
        x0 = 0
        for k, xs in enumerate(DOWN):
            pack_rows(vel, outs[len(UP) - 1 + k], 0, x0)
            x0 += xs


def rest(vel):
    outs = [halo_shape(vel, xs) for xs in UP[1:] + DOWN]
    return pl.pallas_call(
        rest_kernel,
        out_shape=tuple(outs),
        in_specs=in_vmem(1),
        out_specs=in_vmem(len(outs)),
        compiler_params=pltpu.CompilerParams(vmem_limit_bytes=4 << 20),
        name="rest",
    )(vel)


def ends_kernel(vel, right, left, chip):
    n, tile = vel.shape[1], vel.shape[3]
    pack_rows(vel, chip, (1 - parity()) * (tile - 3), 0)

    def step(i, carry):
        _, p, _, t = carry
        return (p, vel[:, i] + R * p, t, vel[:, n - 1 - i] + R * t)

    def steps(b, carry):
        for j in range(8):
            carry = step(b * 8 + j, carry)
        return carry

    carry = (vel[:, 0], vel[:, 0], vel[:, n - 1], vel[:, n - 1])
    for i in range(1, 8):
        carry = step(i, carry)
    p_old, p, t_old, t = lax.fori_loop(1, n // 8, steps, carry)
    right[0] = p_old
    right[1] = p
    left[0] = GAIN * t
    left[1] = GAIN * (t_old + R * vel[:, 0])


def ends(vel):
    comps, nx, halves, tile, lanes = vel.shape
    out = pltpu.VMEM((2, comps, halves, tile, lanes), jnp.float32)
    return pl.pallas_call(
        ends_kernel,
        out_shape=(out, out, halo_shape(vel, nx)),
        in_specs=in_vmem(1),
        out_specs=in_vmem(3),
        compiler_params=pltpu.CompilerParams(vmem_limit_bytes=4 << 20),
        name="ends",
    )(vel)


def inner_kernel(vel, chip, zmat, ymat, adv):
    comps, n, halves, tile, lanes = vel.shape
    side = 1 - parity()

    def block(b, _):
        rows = pl.ds(b * XB, XB)
        sv = rows_of(vel, 1, rows) * (-1.0 / 60.0)
        sw = rows_of(vel, 2, rows) * (-1.0 / 60.0)
        size = XB * tile
        parts = [split(rows_of(vel, c, rows)) for c in range(comps)]
        stack = [p[0] for p in parts] + [p[1] for p in parts]
        gz = dot(jnp.concatenate(stack, axis=0), zmat[...])
        for c in range(comps):
            halo = split(chip[c, :, rows].reshape(-1, halves * lanes))
            gy = [
                dot(ymat[side], jnp.concatenate([p, h], axis=0))
                for p, h in zip(parts[c], halo)
            ]
            low = gz[(comps + c) * size : (comps + c + 1) * size]
            along_z = gz[c * size : (c + 1) * size] + low
            put_rows(adv, c, rows, sv * (gy[0] + gy[1]) + sw * along_z)
        return 0

    lax.fori_loop(0, n // XB, block, 0, unroll=UNROLL)


def inner(vel, chip, zmat, ymat):
    return pl.pallas_call(
        inner_kernel,
        out_shape=pltpu.VMEM(vel.shape, jnp.float32),
        in_specs=in_vmem(4),
        out_specs=pl.BlockSpec(memory_space=pltpu.VMEM),
        compiler_params=pltpu.CompilerParams(vmem_limit_bytes=8 << 20),
        name="inner",
    )(vel, chip, zmat, ymat)


def along_kernel(vel, from_left, from_right, adv_in, adv, deriv_out, deriv, sems):
    n = vel.shape[1]

    def forward(b, p):
        for j in range(EB):
            i = b * EB + j
            p = vel[:, i] + R * p
            deriv[:, i] = p
        return p

    p_left = from_left[1]
    p_end = lax.fori_loop(0, n // EB, forward, p_left)
    h_n = from_right[0] + (GAIN * R) * p_end
    h_n1 = from_right[1] + (GAIN * R * R) * p_end
    h_a = deriv[:, n - 1] + R * h_n
    h_b = deriv[:, n - 2] + R * h_a

    def copy_out(b):
        rows = pl.ds(b * EB, EB)
        return pltpu.make_async_copy(deriv.at[:, rows], deriv_out.at[:, rows], sems.at[b])

    def backward(b, carry, last=False):
        h4, h3, h2, h1 = carry
        for j in range(EB):
            i = b * EB + EB - 1 - j
            if last and i < 2:
                p = p_left if i == 1 else from_left[0]
            else:
                p = deriv[:, i - 2]
            h = p + R * h1
            g = NEAR * (h3 - h1) + FAR * (h4 - h)
            deriv[:, i] = g
            adv[:, i] = adv_in[:, i] - vel[0, i][None] * g
            h4, h3, h2, h1 = h3, h2, h1, h
        copy_out(b).start()
        return (h4, h3, h2, h1)

    blocks = n // EB
    carry = lax.fori_loop(
        0, blocks - 1, lambda k, c: backward(blocks - 1 - k, c), (h_n1, h_n, h_a, h_b)
    )
    backward(0, carry, last=True)
    for b in range(blocks):
        copy_out(b).wait()


def along(vel, from_left, from_right, adv):
    return pl.pallas_call(
        along_kernel,
        out_shape=(
            pltpu.VMEM(vel.shape, jnp.float32),
            jax.ShapeDtypeStruct(vel.shape, jnp.float32),
        ),
        in_specs=in_vmem(4),
        out_specs=[
            pl.BlockSpec(memory_space=pltpu.VMEM),
            pl.BlockSpec(memory_space=pl.ANY),
        ],
        scratch_shapes=[
            pltpu.VMEM(vel.shape, jnp.float32),
            pltpu.SemaphoreType.DMA((vel.shape[1] // EB,)),
        ],
        input_output_aliases={3: 0},
        compiler_params=pltpu.CompilerParams(vmem_limit_bytes=8 << 20),
        name="along",
    )(vel, from_left, from_right, adv)


def outer_kernel(x0, side, sizes, *refs):
    vel, adv_in, hmat = refs[:3]
    pieces = refs[3 : 3 + len(sizes)]
    adv_out, adv, sems = refs[-3:]
    comps, xs, halves, _, lanes = adv.shape

    span = OB if xs <= 32 else 4 * OB

    def take(c, at):
        for size, ref in zip(sizes, pieces):
            if at < size:
                return ref[c, :, at : at + OB].reshape(-1, halves * lanes)
            at -= size

    @pl.when(parity() == side)
    def _():
        copies = []
        for start in range(0, xs, span):
            count = min(span, xs - start)
            for at in range(start, start + count, OB):
                rows = pl.ds(x0 + at, OB)
                sv = rows_of(vel, 1, rows) * (1.0 / 60.0)
                for c in range(comps):
                    gy = split_dot(hmat[side], take(c, at))
                    put_rows(
                        adv, c, pl.ds(at, OB), rows_of(adv_in, c, rows) - sv * gy
                    )
            copies.append(
                pltpu.make_async_copy(
                    adv.at[:, pl.ds(start, count)],
                    adv_out.at[:, pl.ds(x0 + start, count)],
                    sems.at[start // span],
                )
            )
            copies[-1].start()
        for cp in copies:
            cp.wait()


def outer(vel, adv, hmat, pieces, x0, side, out):
    comps, _, halves, tile, lanes = vel.shape
    sizes = tuple(x.shape[2] for x in pieces)
    xs = sum(sizes)
    args = [vel, adv, hmat, *pieces]
    specs = in_vmem(len(args))
    alias = {}
    if out is not None:
        alias = {len(args): 0}
        args.append(out)
        specs.append(pl.BlockSpec(memory_space=pl.ANY))
    return pl.pallas_call(
        functools.partial(outer_kernel, x0, side, sizes),
        out_shape=jax.ShapeDtypeStruct(vel.shape, jnp.float32),
        in_specs=specs,
        out_specs=pl.BlockSpec(memory_space=pl.ANY),
        scratch_shapes=[
            pltpu.VMEM((comps, xs, halves, tile, lanes), jnp.float32),
            pltpu.SemaphoreType.DMA((4,)),
        ],
        input_output_aliases=alias,
        compiler_params=pltpu.CompilerParams(vmem_limit_bytes=8 << 20),
        name="outer",
    )(*args)


def send(x, axis, starts, step):
    count = lax.axis_size(axis)
    return lax.ppermute(x, axis, [(i, (i + s) % count) for i, s in zip(starts, step)])


def shift(x, axis, step):
    count = lax.axis_size(axis)
    return send(x, axis, range(count), [step] * count)


def swap(x, axis):
    count = lax.axis_size(axis)
    return send(x, axis, range(count), [1, -1] * (count // 2))


def on_device(velocity):
    comps, nx, tile, nz = velocity.shape
    halves = nz // LANES
    zmat = jnp.asarray(z_matrix(nz), jnp.bfloat16)
    both = [np.concatenate([y_matrix(tile, XB), m], 1) for m in halo_matrices(tile, XB)]
    ymat = jnp.asarray(np.stack(both), jnp.bfloat16)
    omat = jnp.asarray(halo_matrices(tile, OB), jnp.bfloat16)
    vel = velocity.reshape(comps, nx, tile, halves, LANES).transpose(0, 1, 3, 2, 4)
    up = [first(vel, UP[0])]
    sends = rest(vel)
    up += sends[: len(UP) - 1]
    down = sends[len(UP) - 1 :]
    lows = [shift(x, "cross", 1) for x in up]
    highs = [shift(x, "cross", -1) for x in down]
    right, left, chip = ends(vel)
    chip = swap(chip, "cross")
    from_left = shift(right, "line", 1)
    from_right = shift(left, "line", -1)
    adv = inner(vel, chip, zmat, ymat)
    adv, deriv = along(vel, from_left, from_right, adv)
    out = None
    for side, parts, stages in ((0, lows, UP_STAGES), (1, highs, DOWN_STAGES)):
        for x0, which in stages:
            out = outer(vel, adv, omat, [parts[k] for k in which], x0, side, out)
    return tuple(
        v.transpose(0, 1, 3, 2, 4).reshape(velocity.shape) for v in (out, deriv)
    )


def solution(mesh):
    spec = P(None, "line", "cross", None)
    return jax.shard_map(
        on_device,
        mesh=mesh,
        in_specs=(spec,),
        out_specs=(spec, spec),
        check_vma=False,
    )
```
